256 devices in a mesh: sky: 32 (over x, z), band: 8 (over y, core).
Axes of the slice: x: 4, y: 4, z: 8, core: 2. Of those that a mesh axis runs over, the one named last changes fastest.
Arguments:
- residual_start: float32 [8, 32, 256, 256], P('band', 'sky'), may hold values from -6 to 6
- beam_pattern: float32 [8, 256, 256], P('band'), may hold values from -0.046875 to 0.046875
- spec_weights: float32 [8, 3], replicated, may hold values from -1 to 1
- thresholds: float32 [4, 3], replicated, may hold values from 0.3 to 1.5
- block_ids: int32 [8, 32, 4], P('band', 'sky'), may hold values from 0 to 3, each once within a row
- block_counts: int32 [8, 32], P('band', 'sky'), may hold values from 0 to 4, as said below
Outputs:
- model_coeffs: float32 [3, 32, 256, 256], P(None, 'sky', 'band')
- residual_final: float32 [8, 32, 256, 256], P('band', 'sky')
The draws below stay inside these ranges and needn't reach their ends.
Inputs may be any that keep to these rules, and one draw needn't show every extreme that they name: `block_ids`: each list names every block of its tile once. `block_counts`: every subband has a tile with all 4 blocks occupied.
All inputs are finite; a program needn't handle non-finite values.
Results may differ from the reference program's by a relative error of at most 0.00014.
Values sent between devices are 32-bit elements; how exact they have to be, the bound alone decides.
A program may use at most 64 MiB of HBM per device.

```python
import math
import jax
import jax.numpy as jnp
from jax import lax

TILE = 256
PSFW = 256
NCOEF = 3
SCALES = 4
CYCLES = 2
BPT = 4
TGX = 4
BLOCK = 128
NSUB = 8
TILES = 32


def draw_block_counts(key, part):
    key_base, key_hot, key_full = jax.random.split(key, 3)
    baseline = jax.random.randint(key_base, (NSUB, TILES), 0, 3)
    bright = jax.random.randint(key_hot, (NSUB, TILES), 0, 4) == 0
    counts = jnp.minimum(baseline + jnp.where(bright, 2, 0), BPT)
    chosen = jax.random.randint(key_full, (NSUB, 1), 0, TILES)
    counts = jnp.where(jnp.arange(TILES)[None, :] == chosen, BPT, counts)
    return counts.astype(jnp.int32)


def block_levels(own_key, extent, cuts, low, top_value):
    def one(axis_at, shards_of):
        draws = jax.random.uniform(jax.random.fold_in(jax.random.fold_in(own_key, 6), axis_at), (shards_of,), jnp.float32, low / len(cuts), top_value / len(cuts))
        return jnp.repeat(jnp.exp(draws), extent[axis_at] // shards_of).reshape((-1,) + (1,) * (len(extent) - axis_at - 1))

    level = one(*cuts[0])
    for cut in cuts[1:]:
        level = level * one(*cut)
    return level


def gaussian(own_key, shape, scale, limit, cuts=(), kind=jnp.bfloat16):
    factor_of = block_levels(own_key, shape, cuts, -0.22, 0.18) if cuts else 1.0
    entries = jax.random.normal(own_key, shape, jnp.float32) * scale * factor_of
    return jnp.minimum(jnp.maximum(entries, -limit), limit).astype(kind)


def setup_inputs(seed: int = 0) -> dict:
    splits = jax.random.split(jax.random.key(seed), 7)
    residual_start = gaussian(splits[0], (NSUB, TILES, TILE, TILE), 1.0, 6.0, ((0, 8), (1, 32)), jnp.float32)
    beam_pattern = gaussian(splits[1], (NSUB, PSFW, PSFW), (1.0 / BLOCK), 0.046875, ((0, 8),), jnp.float32)
    spec_weights = jnp.clip(jax.random.uniform(splits[2], (NSUB, NCOEF), jnp.float32, -1.0, 1.0), -1.0, 1.0)
    thresholds = jnp.clip(jnp.exp(jax.random.uniform(splits[3], (SCALES, NCOEF), jnp.float32, math.log(0.3), math.log(1.5))), 0.3, 1.5)
    block_ids = jax.vmap(lambda own: jax.random.permutation(own, BPT))(jax.random.split(splits[4], NSUB * TILES)).reshape((NSUB, TILES, BPT)).astype(jnp.int32)
    block_counts = draw_block_counts(jax.random.fold_in(splits[6], 71), 0)
    return dict(residual_start=residual_start, beam_pattern=beam_pattern, spec_weights=spec_weights, thresholds=thresholds, block_ids=block_ids, block_counts=block_counts)


loop_gain = 0.25
highest = lax.Precision.HIGHEST

def smoothers():
    position = jnp.arange(TILE, dtype=jnp.float32)
    offset = position[:, None] - position[None, :]
    stacked = []
    for scale_pos in range(SCALES):
        spread = 2.0 ** scale_pos * TILE / 16.0
        kernel = jnp.exp(-offset * offset / (2.0 * spread * spread))
        stacked.append(kernel / jnp.sqrt(lax.optimization_barrier(jnp.sum(kernel * kernel, axis=1, keepdims=True))))
    return jnp.stack(stacked)

def make_mask(block_ids, block_counts):
    slot_pos = jnp.arange(BPT, dtype=jnp.int32)
    within = slot_pos[None, None, :] < block_counts[:, :, None]
    matches = block_ids[:, :, :, None] == slot_pos[None, None, None, :]
    live_flags = lax.optimization_barrier(jnp.sum(jnp.where(within[:, :, :, None] & matches, 1.0, 0.0), axis=2)).astype(jnp.float32)
    block_grid = live_flags.reshape(NSUB, TILES, 2, 1, 2, 1)
    expanded = jnp.broadcast_to(block_grid, (NSUB, TILES, 2, BLOCK, 2, BLOCK))
    return expanded.reshape(NSUB, TILES, TILE, TILE)

def convolve(sub_images, beam_pattern):
    rows_grid = TILES // TGX
    height = rows_grid * TILE
    breadth = TGX * TILE
    window = sub_images.reshape(NSUB, rows_grid, TGX, TILE, TILE).transpose(0, 1, 3, 2, 4).reshape(NSUB, height, breadth)
    margin = PSFW // 2
    shape_full = (height + PSFW, breadth + PSFW)

    def single(operands):
        picture, kernel = operands
        spectrum = jnp.fft.rfft2(picture, s=shape_full) * jnp.fft.rfft2(kernel, s=shape_full)
        linear = jnp.fft.irfft2(spectrum, s=shape_full)
        return linear[margin:margin + height, margin:margin + breadth]
    result = lax.map(single, (window, beam_pattern))
    return result.reshape(NSUB, rows_grid, TILE, TGX, TILE).transpose(0, 1, 3, 2, 4).reshape(NSUB, TILES, TILE, TILE)

def reference(residual_start, beam_pattern, spec_weights, thresholds, block_ids, block_counts):
    smooth = smoothers()
    block_mask = make_mask(block_ids, block_counts)
    residual = residual_start
    model_maps = jnp.zeros((NCOEF, TILES, TILE, TILE), jnp.float32)
    for cycle_pos in range(CYCLES):
        spectral = jnp.einsum('bk,btyx->ktyx', spec_weights, residual, precision=highest)
        update = jnp.zeros_like(model_maps)
        for scale_pos in range(SCALES):
            smoothed = jnp.einsum('yi,ktix->ktyx', smooth[scale_pos], spectral, precision=highest)
            smoothed = jnp.einsum('ktyi,xi->ktyx', smoothed, smooth[scale_pos], precision=highest)
            cutoff = thresholds[scale_pos][:, None, None, None]
            update = update + smoothed - jnp.clip(smoothed, -cutoff, cutoff)
        update = loop_gain * update
        model_maps = model_maps + update
        sub_images = jnp.einsum('bk,ktyx->btyx', spec_weights, update, precision=highest) * block_mask
        residual = residual - convolve(sub_images, beam_pattern)
    return (model_maps, residual)
```

```python
import functools

import jax
import jax.numpy as jnp
import numpy as np
from jax import lax
from jax.experimental import pallas as pl
from jax.experimental.pallas import tpu as pltpu
from jax.sharding import PartitionSpec as P

CYCLES = 2
TGX = 4
GAIN = 0.25
RANK = 42
KPAD = 48
FLAG_ROW = 44
MESH = pl.DeviceIdType.MESH
BF = jnp.bfloat16
F32 = jnp.float32


def host_split(a):
    hi = np.asarray(a, np.float64).astype(BF)
    lo = (np.asarray(a, np.float64) - hi.astype(np.float64)).astype(BF)
    return hi, lo


def host_tables(tile, levels):
    pos = np.arange(tile, dtype=np.float64)
    off = pos[:, None] - pos[None, :]
    smooth = []
    for j in range(levels):
        spread = 2.0**j * tile / 16.0
        k = np.exp(-off * off / (2.0 * spread * spread))
        smooth.append(k / np.sqrt(np.sum(k * k, axis=1, keepdims=True)))
    smooth = np.stack(smooth)
    _, _, vt = np.linalg.svd(smooth.reshape(-1, tile), full_matrices=False)
    basis = vt[:RANK].T
    proj = np.zeros((tile, 128))
    proj[:, :RANK] = basis
    proj_t = np.zeros((KPAD, tile))
    proj_t[:RANK] = basis.T
    expand = smooth @ basis
    half = tile // 2

    p_hi, p_lo = host_split(proj)
    t_hi, t_lo = host_split(proj_t)
    project = np.concatenate([p_hi, p_hi, p_lo], axis=0)
    project_t = np.concatenate([t_hi, t_hi, t_lo], axis=1)

    left = np.zeros((levels, tile, KPAD))
    left[:, :, :RANK] = expand
    l_hi, l_lo = host_split(left)
    left3 = np.concatenate([l_hi, l_hi, l_lo], axis=2)

    right = np.zeros((levels, 128, 6 * half))
    for k in range(3):
        for h in range(2):
            at = (3 * h + k) * half
            right[:, RANK * k : RANK * (k + 1), at : at + half] = expand[
                :, h * half : (h + 1) * half
            ].transpose(0, 2, 1)
    r_hi, r_lo = host_split(right)
    right3 = np.concatenate([r_hi, r_lo], axis=1)

    n = 2 * tile
    f = np.arange(tile) + 0.5
    samp = np.arange(n)
    ang = 2.0 * np.pi * f[:, None] * samp[None, :] / n
    rows_f = np.concatenate([np.cos(ang), -np.sin(ang)], axis=0)
    f_hi, f_lo = host_split(rows_f)
    rows_fwd = np.stack([f_hi, f_lo])
    ang_out = ang[:, tile:].T
    rows_i = np.concatenate([np.cos(ang_out), -np.sin(ang_out)], axis=1) * (2.0 / (n * n))
    i_hi, i_lo = host_split(rows_i)
    rows_inv = np.stack([i_hi, i_lo])

    fwd, inv = [], []
    x = np.arange(tile)
    for parity in range(2):
        a = 2.0 * np.pi * x[:, None] * (2 * np.arange(tile)[None, :] + parity) / n
        c, s = np.cos(a), np.sin(a)
        sign = 1.0 - 2.0 * parity
        fwd.append(np.stack(host_split(np.concatenate([c, s], axis=0))))
        inv.append(np.stack(host_split(sign * np.concatenate([c.T, s.T], axis=0))))
    cols_fwd, cols_inv = np.stack(fwd), np.stack(inv)
    return project, project_t, left3, right3, rows_fwd, rows_inv, cols_fwd, cols_inv


def split(v):
    hi = v.astype(BF)
    return hi, (v - hi.astype(F32)).astype(BF)


def dot(a, b):
    return jnp.dot(a, b, preferred_element_type=F32)


def data_const(hi, lo, c_hi, c_lo):
    return dot(jnp.concatenate([hi, lo, hi], axis=1), jnp.concatenate([c_hi, c_hi, c_lo], axis=0))


def const_data(c_hi, c_lo, hi, lo):
    return dot(jnp.concatenate([c_hi, c_hi, c_lo], axis=1), jnp.concatenate([hi, lo, hi], axis=0))


def soft(v, t):
    return v - jnp.minimum(jnp.maximum(v, -t), t)


def rotate(hi, lo):
    half = hi.shape[0] // 2

    def one(v):
        return jnp.concatenate(
            [
                jnp.concatenate([v[:half], v[half:]], axis=1),
                jnp.concatenate([v[half:], -v[:half]], axis=1),
            ],
            axis=0,
        )

    return one(hi), one(lo)


SLOTS = [(dr, dc) for dr in (-1, 0, 1) for dc in (-1, 0, 1)]


def kernel(
    bands,
    sky,
    ids_ref,
    count_ref,
    weight_ref,
    thr_ref,
    res_in,
    beam_ref,
    project_hbm,
    project_t_hbm,
    left_hbm,
    right_hbm,
    rows_fwd_hbm,
    rows_inv_hbm,
    cols_fwd_hbm,
    cols_inv_hbm,
    model_out,
    res_out,
    project,
    project_t,
    left,
    right,
    rows_fwd,
    rows_inv,
    cols_fwd,
    cols_inv,
    gather,
    sky_buf,
    coef3,
    own3,
    u_hi,
    u_lo,
    win,
    win_hi,
    win_lo,
    beam_f,
    sd_hi,
    sd_lo,
    z_acc,
    const_sem,
    band_send,
    band_recv,
    sky_send,
    sky_recv,
):
    tile = res_in.shape[0]
    half = tile // 2
    levels = left.shape[0]
    slab = tile // bands
    sky_rows = sky // TGX
    me = lax.axis_index("band")
    spot = lax.axis_index("sky")
    row, col = spot // TGX, spot % TGX

    def sky_id(dr, dc):
        return ((row + dr + sky_rows) % sky_rows) * TGX + (col + dc + TGX) % TGX

    pairs = [
        (project_t_hbm, project_t),
        (project_hbm, project),
        (rows_fwd_hbm, rows_fwd),
        (cols_fwd_hbm, cols_fwd),
        (left_hbm, left),
        (right_hbm, right),
        (cols_inv_hbm, cols_inv),
        (rows_inv_hbm, rows_inv),
    ]
    copies = [
        pltpu.make_async_copy(src, dst, const_sem.at[i]) for i, (src, dst) in enumerate(pairs)
    ]
    for copy in copies:
        copy.start()

    barrier = pltpu.get_barrier_semaphore()
    for d in range(1, bands):
        pl.semaphore_signal(
            barrier, inc=1, device_id={"band": (me + d) % bands}, device_id_type=MESH
        )
    for dr, dc in SLOTS:
        if (dr, dc) != (0, 0):
            pl.semaphore_signal(
                barrier, inc=1, device_id={"sky": sky_id(dr, dc)}, device_id_type=MESH
            )
    pl.semaphore_wait(barrier, bands - 1 + 8)

    res_out[...] = res_in[...]
    model_out[...] = jnp.zeros_like(model_out)
    copies[0].wait()
    copies[1].wait()

    lane = lax.broadcasted_iota(jnp.int32, (1, 128), 1)
    lane16 = lax.broadcasted_iota(jnp.int32, (16, 128), 1)
    row48 = lax.broadcasted_iota(jnp.int32, (KPAD, 128), 0)
    flags = []
    for q in range(4):
        live = jnp.float32(0.0)
        for s in range(4):
            hit = jnp.where(ids_ref[s] == q, 1.0, 0.0) * jnp.where(s < count_ref[0], 1.0, 0.0)
            live = live + hit
        flags.append(live)
    weights = [weight_ref[me, k] for k in range(3)]
    scale = jnp.zeros((1, 128), F32)
    for k in range(3):
        inside = (lane >= RANK * k) & (lane < RANK * (k + 1))
        scale = jnp.where(inside, GAIN * weights[k], scale)

    def band_copy(cyc, d):
        return pltpu.make_async_remote_copy(
            src_ref=gather.at[cyc, 0],
            dst_ref=gather.at[cyc, d],
            send_sem=band_send.at[cyc, d],
            recv_sem=band_recv.at[cyc, d],
            device_id={"band": (me + d) % bands},
            device_id_type=MESH,
        )

    def sky_copy(cyc, dr, dc):
        slot = (1 - dr) * 3 + (1 - dc)
        return pltpu.make_async_remote_copy(
            src_ref=sky_buf.at[cyc, 4],
            dst_ref=sky_buf.at[cyc, slot],
            send_sem=sky_send.at[cyc, slot],
            recv_sem=sky_recv.at[cyc, slot],
            device_id={"sky": sky_id(dr, dc)},
            device_id_type=MESH,
        )

    def valid(dr, dc):
        good = (row + dr >= 0) & (row + dr < sky_rows) & (col + dc >= 0) & (col + dc < TGX)
        return jnp.where(good, 1.0, 0.0)

    def cycle(cyc, carry):
        r_hi, r_lo = split(res_out[...])
        part = dot(project_t[...], jnp.concatenate([r_hi, r_lo, r_hi], axis=0))
        p_hi, p_lo = split(part)
        coef = dot(jnp.concatenate([p_hi, p_lo, p_hi], axis=1), project[...])
        gather[cyc, 0] = (
            coef[0:16]
            + pltpu.roll(coef[16:32], RANK, 1)
            + pltpu.roll(coef[32:48], 2 * RANK, 1)
        )
        for d in range(1, bands):
            band_copy(cyc, d).start()

        @pl.when(cyc == 0)
        def _():
            copies[2].wait()
            copies[3].wait()
            b_hi, b_lo = split(beam_ref[...])
            first = const_data(rows_fwd[0, :, :tile], rows_fwd[1, :, :tile], b_hi, b_lo)
            l_hi, l_lo = rotate(*split(first))
            for parity in range(2):
                beam_f[parity] = data_const(l_hi, l_lo, cols_fwd[parity, 0], cols_fwd[parity, 1])
            copies[4].wait()
            copies[5].wait()

        for d in range(1, bands):
            band_copy(cyc, d).wait_recv()
        sums = []
        for k in range(3):
            total = weights[k] * gather[cyc, 0]
            for d in range(1, bands):
                total = total + weight_ref[(me - d + bands) % bands, k] * gather[cyc, d]
            sums.append(total)
        groups = []
        for g in range(3):
            out = jnp.zeros((16, 128), F32)
            for k in range(3):
                moved = sums[k]
                if k != g:
                    moved = pltpu.roll(moved, (RANK * (k - g)) % 128, 1)
                inside = (lane16 >= RANK * k) & (lane16 < RANK * (k + 1))
                out = jnp.where(inside, moved, out)
            groups.append(out)
        full = jnp.concatenate(groups, axis=0)
        for q in range(4):
            full = jnp.where(row48 == FLAG_ROW + q, flags[q], full)
        sky_buf[cyc, 4] = full
        for dr, dc in SLOTS:
            if (dr, dc) != (0, 0):
                sky_copy(cyc, dr, dc).start()

        o_hi, o_lo = split(full)
        own3[...] = jnp.concatenate([o_hi, o_lo, o_hi], axis=0)
        for dr, dc in SLOTS:
            if (dr, dc) != (0, 0):
                sky_copy(cyc, dr, dc).wait_recv()
        for dr, dc in SLOTS:
            c_hi, c_lo = split(
                sky_buf[cyc, (dr + 1) * 3 + dc + 1] * (scale * valid(dr, dc))
            )
            coef3[dr + 1, :, (dc + 1) * 128 : (dc + 2) * 128] = jnp.concatenate(
                [c_hi, c_lo, c_hi], axis=0
            )
        win[...] = jnp.zeros_like(win)

        def level(j, carry):
            for tr, (src, n, dst) in enumerate(
                ((half, half, 0), (0, tile, half), (0, half, half + tile))
            ):
                hi, lo = split(dot(left[j, src : src + n, :], coef3[tr]))
                u_hi[dst : dst + n, :] = hi
                u_lo[dst : dst + n, :] = lo
            at = pl.multiple_of(me * slab, slab)
            e_hi, e_lo = split(dot(left[j, pl.ds(at, slab), :], own3[...]))
            cut = [GAIN * jnp.abs(weights[k]) * thr_ref[j, k] for k in range(3)]
            raw = [thr_ref[j, k] for k in range(3)]

            def spread(hi, lo, h):
                c_hi = right[j, 0:128, 384 * h : 384 * (h + 1)]
                c_lo = right[j, 128:256, 384 * h : 384 * (h + 1)]
                return data_const(hi, lo, c_hi, c_lo)

            for h in range(2):
                got = spread(
                    jnp.concatenate([u_hi[:, 128:256], e_hi], axis=0),
                    jnp.concatenate([u_lo[:, 128:256], e_lo], axis=0),
                    h,
                )
                new = win[:, half * (1 + h) : half * (2 + h)]
                for k in range(3):
                    block = got[:, 128 * k : 128 * (k + 1)]
                    new = new + soft(block[: 2 * tile], cut[k])
                    model_out[k, :, half * h : half * (h + 1)] += GAIN * soft(
                        block[2 * tile :], raw[k]
                    )
                win[:, half * (1 + h) : half * (2 + h)] = new
            for side in range(2):
                lanes = slice(256 * side, 256 * side + 128)
                got = spread(u_hi[:, lanes], u_lo[:, lanes], 1 - side)
                cols = slice(3 * half * side, 3 * half * side + half)
                new = win[:, cols]
                for k in range(3):
                    new = new + soft(got[:, 128 * k : 128 * (k + 1)], cut[k])
                win[:, cols] = new
            return carry

        lax.fori_loop(0, levels, level, 0)

        for rb in range(4):
            tr, qr = ((-1, 1), (0, 0), (0, 1), (1, 0))[rb]
            for cb in range(4):
                tc, qc = ((-1, 1), (0, 0), (0, 1), (1, 0))[cb]
                at = FLAG_ROW + 2 * qr + qc
                flag = sky_buf[cyc, (tr + 1) * 3 + tc + 1, at : at + 1, :]
                rows, cols = slice(half * rb, half * (rb + 1)), slice(half * cb, half * (cb + 1))
                hi, lo = split(win[rows, cols] * flag)
                win_hi[rows, cols] = hi
                win_lo[rows, cols] = lo

        spec = const_data(rows_fwd[0], rows_fwd[1], win_hi[...], win_lo[...])
        near, far = spec[:, :tile], spec[:, tile:]
        for parity, v in enumerate((near + far, near - far)):
            hi, lo = split(v)
            sd_hi[parity] = hi
            sd_lo[parity] = lo

        @pl.when(cyc == 0)
        def _():
            copies[6].wait()
            copies[7].wait()

        z_acc[...] = jnp.zeros_like(z_acc)

        def column(parity, carry):
            hi, lo = rotate(sd_hi[parity], sd_lo[parity])
            x = data_const(hi, lo, cols_fwd[parity, 0], cols_fwd[parity, 1])
            x_re, x_im = x[:tile], x[tile:]
            b_re, b_im = beam_f[parity, :tile], beam_f[parity, tile:]
            y_re = x_re * b_re - x_im * b_im
            y_im = x_re * b_im + x_im * b_re
            r_hi, r_lo = split(y_re)
            i_hi, i_lo = split(y_im)

            def stack(re, im):
                return jnp.concatenate(
                    [jnp.concatenate([re, -im], axis=1), jnp.concatenate([im, re], axis=1)],
                    axis=0,
                )

            z_acc[...] += data_const(
                stack(r_hi, i_hi), stack(r_lo, i_lo), cols_inv[parity, 0], cols_inv[parity, 1]
            )
            return carry

        lax.fori_loop(0, 2, column, 0)
        z_hi, z_lo = split(z_acc[...])
        res_out[...] = res_out[...] - const_data(rows_inv[0], rows_inv[1], z_hi, z_lo)
        for d in range(1, bands):
            band_copy(cyc, d).wait_send()
        for dr, dc in SLOTS:
            if (dr, dc) != (0, 0):
                sky_copy(cyc, dr, dc).wait_send()
        return carry

    lax.fori_loop(0, CYCLES, cycle, 0)


def on_device(residual_start, beam_pattern, spec_weights, thresholds, block_ids, block_counts):
    bands = lax.axis_size("band")
    sky = lax.axis_size("sky")
    tile = residual_start.shape[-1]
    coefs = spec_weights.shape[1]
    levels = thresholds.shape[0]
    tables = host_tables(tile, levels)
    smem = pl.BlockSpec(memory_space=pltpu.SMEM)
    vmem = pl.BlockSpec(memory_space=pltpu.VMEM)
    hbm = pl.BlockSpec(memory_space=pl.ANY)
    region = 2 * tile
    model, res = pl.pallas_call(
        functools.partial(kernel, bands, sky),
        out_shape=(
            jax.ShapeDtypeStruct((coefs, tile // bands, tile), F32),
            jax.ShapeDtypeStruct((tile, tile), F32),
        ),
        in_specs=[smem] * 4 + [vmem] * 2 + [hbm] * 8,
        out_specs=(vmem, vmem),
        scratch_shapes=[pltpu.VMEM(t.shape, BF) for t in tables]
        + [
            pltpu.VMEM((CYCLES, bands, 16, 128), F32),
            pltpu.VMEM((CYCLES, 9, KPAD, 128), F32),
            pltpu.VMEM((3, 3 * KPAD, 384), BF),
            pltpu.VMEM((3 * KPAD, 128), BF),
            pltpu.VMEM((region, 384), BF),
            pltpu.VMEM((region, 384), BF),
            pltpu.VMEM((region, region), F32),
            pltpu.VMEM((region, region), BF),
            pltpu.VMEM((region, region), BF),
            pltpu.VMEM((2, region, tile), F32),
            pltpu.VMEM((2, region, tile), BF),
            pltpu.VMEM((2, region, tile), BF),
            pltpu.VMEM((region, tile), F32),
            pltpu.SemaphoreType.DMA((8,)),
            pltpu.SemaphoreType.DMA((CYCLES, bands)),
            pltpu.SemaphoreType.DMA((CYCLES, bands)),
            pltpu.SemaphoreType.DMA((CYCLES, 9)),
            pltpu.SemaphoreType.DMA((CYCLES, 9)),
        ],
        compiler_params=pltpu.CompilerParams(
            collective_id=0, has_side_effects=True, vmem_limit_bytes=56 << 20
        ),
    )(
        block_ids[0, 0],
        block_counts[0],
        spec_weights,
        thresholds,
        residual_start[0, 0],
        beam_pattern[0],
        *[jnp.asarray(t) for t in tables],
    )
    return (model[:, None], res[None, None])


def solution(mesh):
    placed = (
        P("band", "sky", None, None),
        P("band", None, None),
        P(),
        P(),
        P("band", "sky", None),
        P("band", "sky"),
    )
    return jax.shard_map(
        on_device,
        mesh=mesh,
        in_specs=placed,
        out_specs=(P(None, "sky", "band", None), P("band", "sky", None, None)),
        check_vma=False,
    )
```

```python
import functools

import jax
import jax.numpy as jnp
import numpy as np
from jax import lax
from jax.experimental import pallas as pl
from jax.experimental.pallas import tpu as pltpu
from jax.sharding import PartitionSpec as P

CYCLES = 2
TGX = 4
GAIN = 0.25
RANK = 42
KPAD = 48
FLAG_ROW = 44
MESH = pl.DeviceIdType.MESH
BF = jnp.bfloat16
F32 = jnp.float32


def host_split(a):
    hi = np.asarray(a, np.float64).astype(BF)
    lo = (np.asarray(a, np.float64) - hi.astype(np.float64)).astype(BF)
    return hi, lo


def host_tables(tile, levels):
    pos = np.arange(tile, dtype=np.float64)
    off = pos[:, None] - pos[None, :]
    smooth = []
    for j in range(levels):
        spread = 2.0**j * tile / 16.0
        k = np.exp(-off * off / (2.0 * spread * spread))
        smooth.append(k / np.sqrt(np.sum(k * k, axis=1, keepdims=True)))
    smooth = np.stack(smooth)
    _, _, vt = np.linalg.svd(smooth.reshape(-1, tile), full_matrices=False)
    basis = vt[:RANK].T
    proj = np.zeros((tile, 128))
    proj[:, :RANK] = basis
    proj_t = np.zeros((KPAD, tile))
    proj_t[:RANK] = basis.T
    expand = smooth @ basis

    p_hi, p_lo = host_split(proj)
    t_hi, t_lo = host_split(proj_t)
    project = np.concatenate([p_hi, p_hi, p_lo], axis=0)
    project_t = np.concatenate([t_hi, t_hi, t_lo], axis=1)

    left = np.zeros((levels, tile, KPAD))
    left[:, :, :RANK] = expand
    l_hi, l_lo = host_split(left)
    left3 = np.concatenate([l_hi, l_hi, l_lo], axis=2)

    right = np.zeros((levels, 128, tile), BF)
    g_hi, g_lo = host_split(expand.transpose(0, 2, 1))
    for p, g in enumerate((g_hi, g_hi, g_lo)):
        right[:, RANK * p : RANK * (p + 1)] = g

    n = 2 * tile
    f = np.arange(tile) + 0.5
    ang = 2.0 * np.pi * f[:, None] * np.arange(tile)[None, :] / n
    rows_fwd = np.stack(host_split(np.concatenate([np.cos(ang), -np.sin(ang)], axis=0)))

    fwd = []
    x = np.arange(tile)
    for parity in range(2):
        a = 2.0 * np.pi * x[:, None] * (2 * x[None, :] + parity) / n
        fwd.append(np.stack(host_split(np.concatenate([np.cos(a), np.sin(a)], axis=0))))
    cols_fwd = np.stack(fwd)
    return project_t, project, rows_fwd, cols_fwd, left3, right


def split(v):
    hi = v.astype(BF)
    return hi, (v - hi.astype(F32)).astype(BF)


def dot(a, b):
    return jnp.dot(a, b, preferred_element_type=F32)


def data_const(hi, lo, c_hi, c_lo):
    return dot(jnp.concatenate([hi, lo, hi], axis=1), jnp.concatenate([c_hi, c_hi, c_lo], axis=0))


def const_data(c_hi, c_lo, hi, lo):
    return dot(jnp.concatenate([c_hi, c_hi, c_lo], axis=1), jnp.concatenate([hi, lo, hi], axis=0))


def soft(v, t):
    return v - jnp.minimum(jnp.maximum(v, -t), t)


def rotate(hi, lo):
    half = hi.shape[0] // 2

    def one(v):
        return jnp.concatenate(
            [
                jnp.concatenate([v[:half], v[half:]], axis=1),
                jnp.concatenate([v[half:], -v[:half]], axis=1),
            ],
            axis=0,
        )

    return one(hi), one(lo)


NEAR = [(0, 1), (0, -1)]
FAR = [(1, 0), (-1, 0), (1, 1), (1, -1), (-1, 1), (-1, -1)]


def kernel(
    bands,
    sky,
    ids_ref,
    count_ref,
    weight_ref,
    thr_ref,
    res_in,
    beam_hbm,
    project_t_hbm,
    project_hbm,
    rows_hbm,
    cols_hbm,
    left_hbm,
    right_hbm,
    model_out,
    res_out,
    beam,
    project_t,
    project,
    rows_half,
    cols_fwd,
    left,
    right,
    rows_fwd,
    rows_inv,
    cols_odd,
    gather,
    sky_buf,
    coef3,
    own3,
    win,
    spec,
    beam_f,
    sd_hi,
    sd_lo,
    z_acc,
    const_sem,
    band_send,
    band_recv,
    sky_send,
    sky_recv,
):
    tile = res_in.shape[0]
    half = tile // 2
    levels = left.shape[0]
    slab = tile // bands
    sky_rows = sky // TGX
    me = lax.axis_index("band")
    spot = lax.axis_index("sky")
    row, col = spot // TGX, spot % TGX

    def sky_id(dr, dc):
        return ((row + dr + sky_rows) % sky_rows) * TGX + (col + dc + TGX) % TGX

    pairs = [
        (project_t_hbm, project_t),
        (project_hbm, project),
        (beam_hbm, beam),
        (rows_hbm, rows_half),
        (cols_hbm, cols_fwd),
        (left_hbm, left),
        (right_hbm, right),
    ]
    copies = [
        pltpu.make_async_copy(src, dst, const_sem.at[i]) for i, (src, dst) in enumerate(pairs)
    ]
    for copy in copies:
        copy.start()

    barrier = pltpu.get_barrier_semaphore()
    for d in range(1, bands):
        pl.semaphore_signal(
            barrier, inc=1, device_id={"band": (me + d) % bands}, device_id_type=MESH
        )
    for dr, dc in NEAR + FAR:
        pl.semaphore_signal(barrier, inc=1, device_id={"sky": sky_id(dr, dc)}, device_id_type=MESH)

    res_out[...] = res_in[...]
    model_out[...] = jnp.zeros_like(model_out)

    lane = lax.broadcasted_iota(jnp.int32, (1, 128), 1)
    lane16 = lax.broadcasted_iota(jnp.int32, (16, 128), 1)
    row48 = lax.broadcasted_iota(jnp.int32, (KPAD, 128), 0)
    flags = []
    for q in range(4):
        live = jnp.float32(0.0)
        for s in range(4):
            hit = jnp.where(ids_ref[s] == q, 1.0, 0.0) * jnp.where(s < count_ref[0], 1.0, 0.0)
            live = live + hit
        flags.append(live)
    weights = [weight_ref[k, me] for k in range(3)]
    scale = jnp.zeros((1, 128), F32)
    for k in range(3):
        inside = (lane >= RANK * k) & (lane < RANK * (k + 1))
        scale = jnp.where(inside, GAIN * weights[k], scale)

    def band_copy(cyc, d):
        return pltpu.make_async_remote_copy(
            src_ref=gather.at[cyc, 0],
            dst_ref=gather.at[cyc, d],
            send_sem=band_send.at[cyc, d],
            recv_sem=band_recv.at[cyc, d],
            device_id={"band": (me + d) % bands},
            device_id_type=MESH,
        )

    def sky_copy(cyc, dr, dc):
        slot = (1 - dr) * 3 + (1 - dc)
        return pltpu.make_async_remote_copy(
            src_ref=sky_buf.at[cyc, 4],
            dst_ref=sky_buf.at[cyc, slot],
            send_sem=sky_send.at[cyc, slot],
            recv_sem=sky_recv.at[cyc, slot],
            device_id={"sky": sky_id(dr, dc)},
            device_id_type=MESH,
        )

    def valid(dr, dc):
        good = (row + dr >= 0) & (row + dr < sky_rows) & (col + dc >= 0) & (col + dc < TGX)
        return jnp.where(good, 1.0, 0.0)

    def prepare():
        for copy in copies[2:5]:
            copy.wait()
        alt = (1 - 2 * (lax.broadcasted_iota(jnp.int32, (tile, 1), 0) % 2)).astype(F32)
        for part in range(2):
            re = rows_half[part, :tile].astype(F32)
            im = rows_half[part, tile:].astype(F32)
            re_far, im_far = im * alt, -(re * alt)
            rows_fwd[part, :, :tile] = rows_half[part]
            rows_fwd[part, :tile, tile:] = re_far.astype(BF)
            rows_fwd[part, tile:, tile:] = im_far.astype(BF)
            rows_inv[part, :, :tile] = re_far.T.astype(BF)
            rows_inv[part, :, tile:] = im_far.T.astype(BF)
            cols_odd[0, part] = cols_fwd[0, part]
            for h in range(2):
                block = cols_fwd[1, part, h * tile : (h + 1) * tile].astype(F32)
                cols_odd[1, part, h * tile : (h + 1) * tile] = (-block.T).astype(BF)
        b_hi, b_lo = split(beam[...])
        l_hi, l_lo = rotate(*split(const_data(rows_half[0], rows_half[1], b_hi, b_lo)))
        norm = 2.0 / (4 * tile * tile)
        for parity in range(2):
            got = data_const(l_hi, l_lo, cols_fwd[parity, 0], cols_fwd[parity, 1])
            beam_f[parity] = norm * got
        copies[5].wait()
        copies[6].wait()

    def place(cyc, dr, dc):
        c_hi, c_lo = split(sky_buf[cyc, (dr + 1) * 3 + dc + 1] * (scale * valid(dr, dc)))
        coef3[dr + 1, :, (dc + 1) * 128 : (dc + 2) * 128] = jnp.concatenate(
            [c_hi, c_lo, c_hi], axis=0
        )

    def expand(v):
        lanes = lax.broadcasted_iota(jnp.int32, v.shape, 1)
        hi = v.astype(BF).astype(F32)
        lo = v - hi

        def moved(x, by):
            return x if by == 0 else pltpu.roll(x, by % 128, 1)

        out = []
        for k in range(3):
            low = moved(hi, -RANK * k)
            mid = moved(lo, RANK - RANK * k)
            top = moved(hi, 2 * RANK - RANK * k)
            out.append(
                jnp.where(lanes < RANK, low, jnp.where(lanes < 2 * RANK, mid, top)).astype(BF)
            )
        return out

    def smooth(phase, groups):
        win[phase] = jnp.zeros(win.shape[1:], F32)

        def level(j, carry):
            first = jnp.concatenate(
                [dot(left[j, src : src + n, :], coef3[tr]) for src, n, tr in groups], axis=0
            )
            west, mid, east = (expand(first[:, 128 * t : 128 * (t + 1)]) for t in range(3))
            table = right[j]
            blank = jnp.zeros((128, half), BF)
            both = jnp.concatenate(
                [
                    jnp.concatenate([table[:, half:], blank], axis=1),
                    jnp.concatenate([blank, table[:, :half]], axis=1),
                ],
                axis=0,
            )
            cut = [GAIN * jnp.abs(weights[k]) * thr_ref[j, k] for k in range(3)]
            if phase == 0:
                at = pl.multiple_of(me * slab, slab)
                mid = mid + expand(dot(left[j, pl.ds(at, slab), :], own3[...]))
            got = dot(jnp.concatenate(mid, axis=0), table)
            new = win[phase, :, :tile]
            for k in range(3):
                new = new + soft(got[tile * k : tile * (k + 1)], cut[k])
            win[phase, :, :tile] = new
            if phase == 0:
                for k in range(3):
                    block = got[3 * tile + slab * k : 3 * tile + slab * (k + 1)]
                    model_out[k] += GAIN * soft(block, thr_ref[j, k])
            pairs = [jnp.concatenate([west[k], east[k]], axis=1) for k in range(3)]
            got = dot(jnp.concatenate(pairs, axis=0), both)
            new = win[phase, :, tile:]
            for k in range(3):
                new = new + soft(got[tile * k : tile * (k + 1)], cut[k])
            win[phase, :, tile:] = new
            return carry

        lax.fori_loop(0, levels, level, 0)

    def masked(cyc, phase, bands_of_rows):
        rows = []
        for at, (dr, qr) in enumerate(bands_of_rows):
            cols = []
            for (dc, qc), src in (((-1, 1), tile), ((0, 0), 0), ((0, 1), half), ((1, 0), tile + half)):
                f = FLAG_ROW + 2 * qr + qc
                flag = sky_buf[cyc, (dr + 1) * 3 + dc + 1, f : f + 1, :]
                cols.append(win[phase, half * at : half * (at + 1), src : src + half] * flag)
            rows.append(jnp.concatenate(cols, axis=1))
        return split(jnp.concatenate(rows, axis=0))

    def cycle(cyc, carry):
        r_hi, r_lo = split(res_out[...])
        part = dot(project_t[...], jnp.concatenate([r_hi, r_lo, r_hi], axis=0))
        p_hi, p_lo = split(part)
        coef = dot(jnp.concatenate([p_hi, p_lo, p_hi], axis=1), project[...])
        gather[cyc, 0] = (
            coef[0:16] + pltpu.roll(coef[16:32], RANK, 1) + pltpu.roll(coef[32:48], 2 * RANK, 1)
        )

        for d in range(1, bands):
            band_copy(cyc, d).start()

        @pl.when(cyc == 0)
        def _():
            prepare()

        for d in range(1, bands):
            band_copy(cyc, d).wait_recv()
        sums = []
        for k in range(3):
            total = weights[k] * gather[cyc, 0]
            for d in range(1, bands):
                total = total + weight_ref[k, (me - d + bands) % bands] * gather[cyc, d]
            sums.append(total)
        groups = []
        for g in range(3):
            out = jnp.zeros((16, 128), F32)
            for k in range(3):
                moved = sums[k]
                if k != g:
                    moved = pltpu.roll(moved, (RANK * (k - g)) % 128, 1)
                inside = (lane16 >= RANK * k) & (lane16 < RANK * (k + 1))
                out = jnp.where(inside, moved, out)
            groups.append(out)
        full = jnp.concatenate(groups, axis=0)
        for q in range(4):
            full = jnp.where(row48 == FLAG_ROW + q, flags[q], full)
        sky_buf[cyc, 4] = full
        for dr, dc in FAR + NEAR:
            sky_copy(cyc, dr, dc).start()

        o_hi, o_lo = split(full)
        own3[...] = jnp.concatenate([o_hi, o_lo, o_hi], axis=0)
        place(cyc, 0, 0)
        for dr, dc in NEAR:
            sky_copy(cyc, -dr, -dc).wait_recv()
            place(cyc, dr, dc)
        smooth(0, [(0, tile, 1)])
        w_hi, w_lo = masked(cyc, 0, [(0, 0), (0, 1)])
        inner = slice(half, half + tile)
        spec[...] = const_data(rows_fwd[0, :, inner], rows_fwd[1, :, inner], w_hi, w_lo)

        for dr, dc in FAR:
            sky_copy(cyc, -dr, -dc).wait_recv()
            place(cyc, dr, dc)
        smooth(1, [(half, half, 0), (0, half, 2)])
        w_hi, w_lo = masked(cyc, 1, [(-1, 1), (1, 0)])

        def outer(part):
            return jnp.concatenate(
                [rows_fwd[part, :, :half], rows_fwd[part, :, half + tile :]], axis=1
            )

        full_spec = spec[...] + const_data(outer(0), outer(1), w_hi, w_lo)
        near, far = full_spec[:, :tile], full_spec[:, tile:]
        for parity, v in enumerate((near + far, near - far)):
            hi, lo = split(v)
            sd_hi[parity] = hi
            sd_lo[parity] = lo

        z_acc[...] = jnp.zeros_like(z_acc)

        def column(parity, carry):
            hi, lo = rotate(sd_hi[parity], sd_lo[parity])
            x = data_const(hi, lo, cols_fwd[parity, 0], cols_fwd[parity, 1])
            x_re, x_im = x[:tile], x[tile:]
            b_re, b_im = beam_f[parity, :tile], beam_f[parity, tile:]
            y_re = x_re * b_re - x_im * b_im
            y_im = x_re * b_im + x_im * b_re
            r_hi, r_lo = split(y_re)
            i_hi, i_lo = split(y_im)

            def stack(re, im):
                return jnp.concatenate(
                    [jnp.concatenate([re, -im], axis=1), jnp.concatenate([im, re], axis=1)],
                    axis=0,
                )

            z_acc[...] += data_const(
                stack(r_hi, i_hi), stack(r_lo, i_lo), cols_odd[parity, 0], cols_odd[parity, 1]
            )
            return carry

        lax.fori_loop(0, 2, column, 0)
        z_hi, z_lo = split(z_acc[...])
        res_out[...] = res_out[...] - const_data(rows_inv[0], rows_inv[1], z_hi, z_lo)
        for d in range(1, bands):
            band_copy(cyc, d).wait_send()
        for dr, dc in NEAR + FAR:
            sky_copy(cyc, dr, dc).wait_send()
        return carry

    copies[0].wait()
    copies[1].wait()
    pl.semaphore_wait(barrier, bands - 1 + 8)
    lax.fori_loop(0, CYCLES, cycle, 0)


def finish(model_in, res_in, model_out, res_out):
    model_out[...] = model_in[...]
    res_out[...] = res_in[...]


def on_device(residual_start, beam_pattern, spec_weights, thresholds, block_ids, block_counts):
    bands = lax.axis_size("band")
    sky = lax.axis_size("sky")
    tile = residual_start.shape[-1]
    coefs = spec_weights.shape[1]
    levels = thresholds.shape[0]
    tables = host_tables(tile, levels)
    smem = pl.BlockSpec(memory_space=pltpu.SMEM)
    vmem = pl.BlockSpec(memory_space=pltpu.VMEM)
    hbm = pl.BlockSpec(memory_space=pl.ANY)
    region = 2 * tile
    shapes = (
        jax.ShapeDtypeStruct((coefs, tile // bands, tile), F32),
        jax.ShapeDtypeStruct((tile, tile), F32),
    )
    model, res = pl.pallas_call(
        functools.partial(kernel, bands, sky),
        out_shape=shapes,
        in_specs=[smem] * 4 + [vmem] + [hbm] * 7,
        out_specs=(vmem, vmem),
        scratch_shapes=[pltpu.VMEM((tile, tile), F32)]
        + [pltpu.VMEM(t.shape, BF) for t in tables]
        + [
            pltpu.VMEM((2, region, region), BF),
            pltpu.VMEM((2, tile, region), BF),
            pltpu.VMEM((2, 2, region, tile), BF),
            pltpu.VMEM((CYCLES, bands, 16, 128), F32),
            pltpu.VMEM((CYCLES, 9, KPAD, 128), F32),
            pltpu.VMEM((3, 3 * KPAD, 384), BF),
            pltpu.VMEM((3 * KPAD, 128), BF),
            pltpu.VMEM((2, tile, region), F32),
            pltpu.VMEM((region, region), F32),
            pltpu.VMEM((2, region, tile), F32),
            pltpu.VMEM((2, region, tile), BF),
            pltpu.VMEM((2, region, tile), BF),
            pltpu.VMEM((region, tile), F32),
            pltpu.SemaphoreType.DMA((7,)),
            pltpu.SemaphoreType.DMA((CYCLES, bands)),
            pltpu.SemaphoreType.DMA((CYCLES, bands)),
            pltpu.SemaphoreType.DMA((CYCLES, 9)),
            pltpu.SemaphoreType.DMA((CYCLES, 9)),
        ],
        compiler_params=pltpu.CompilerParams(
            collective_id=0, has_side_effects=True, vmem_limit_bytes=32 << 20
        ),
    )(
        block_ids[0, 0],
        block_counts[0],
        spec_weights.T,
        thresholds,
        *[
            pltpu.with_memory_space_constraint(x, pltpu.HBM)
            for x in (
                residual_start[0, 0],
                beam_pattern[0],
                *[jnp.asarray(t) for t in tables],
            )
        ],
    )
    model, res = pl.pallas_call(
        finish,
        out_shape=shapes,
        in_specs=[vmem] * 2,
        out_specs=(vmem, vmem),
        compiler_params=pltpu.CompilerParams(vmem_limit_bytes=4 << 20),
    )(model, res)
    return (model[:, None], res[None, None])


def solution(mesh):
    placed = (
        P("band", "sky", None, None),
        P("band", None, None),
        P(),
        P(),
        P("band", "sky", None),
        P("band", "sky"),
    )
    return jax.shard_map(
        on_device,
        mesh=mesh,
        in_specs=placed,
        out_specs=(P(None, "sky", "band", None), P("band", "sky", None, None)),
        check_vma=False,
    )
```

```python
import functools

import jax
import jax.numpy as jnp
import numpy as np
from jax import lax
from jax.experimental import pallas as pl
from jax.experimental.pallas import tpu as pltpu
from jax.sharding import PartitionSpec as P

CYCLES = 2
TGX = 4
GAIN = 0.25
RANK = 42
KPAD = 48
FAR_RANK = 32
MESH = pl.DeviceIdType.MESH
BF = jnp.bfloat16
F32 = jnp.float32


def host_split(a):
    hi = np.asarray(a, np.float64).astype(BF)
    lo = (np.asarray(a, np.float64) - hi.astype(np.float64)).astype(BF)
    return hi, lo


def host_tables(tile, levels):
    pos = np.arange(tile, dtype=np.float64)
    off = pos[:, None] - pos[None, :]
    smooth = []
    for j in range(levels):
        spread = 2.0**j * tile / 16.0
        k = np.exp(-off * off / (2.0 * spread * spread))
        smooth.append(k / np.sqrt(np.sum(k * k, axis=1, keepdims=True)))
    smooth = np.stack(smooth)
    _, _, vt = np.linalg.svd(smooth.reshape(-1, tile), full_matrices=False)
    basis = vt[:RANK].T
    proj = np.zeros((tile, 128))
    proj[:, :RANK] = basis
    proj_t = np.zeros((KPAD, tile))
    proj_t[:RANK] = basis.T
    expand = smooth @ basis

    p_hi, p_lo = host_split(proj)
    t_hi, t_lo = host_split(proj_t)
    project = np.concatenate([p_hi, p_hi, p_lo], axis=0)
    project_t = np.concatenate([t_hi, t_hi, t_lo], axis=1)

    left = np.zeros((levels, tile, KPAD))
    left[:, :, :RANK] = expand
    l_hi, l_lo = host_split(left)
    left3 = np.concatenate([l_hi, l_hi, l_lo], axis=2)

    far, reduce = [], np.zeros((2 * FAR_RANK, KPAD))
    for i, rows in enumerate((slice(tile // 2, tile), slice(0, tile // 2))):
        _, _, vt = np.linalg.svd(expand[:, rows].reshape(-1, RANK), full_matrices=False)
        reduce[FAR_RANK * i : FAR_RANK * (i + 1), :RANK] = vt[:FAR_RANK]
        f_hi, f_lo = host_split(expand[:, rows] @ vt[:FAR_RANK].T)
        far.append(np.concatenate([f_hi, f_hi, f_lo], axis=2))
    left_far = np.stack(far, axis=1)
    z_hi, z_lo = host_split(reduce)
    reduce3 = np.concatenate([z_hi, z_hi, z_lo], axis=1)

    right = np.zeros((levels, 128, tile), BF)
    g_hi, g_lo = host_split(expand.transpose(0, 2, 1))
    for p, g in enumerate((g_hi, g_hi, g_lo)):
        right[:, RANK * p : RANK * (p + 1)] = g

    n = 2 * tile
    f = np.arange(tile) + 0.5
    ang = 2.0 * np.pi * f[:, None] * np.arange(tile)[None, :] / n
    rows_fwd = np.stack(host_split(np.concatenate([np.cos(ang), -np.sin(ang)], axis=0)))

    cols = []
    x = np.arange(tile // 2)
    for r in range(4):
        a = 2.0 * np.pi * x[:, None] * (4 * x[None, :] + r) / n
        c, s = np.cos(a), np.sin(a)
        cols.append(np.stack(host_split(np.block([[c, -s], [s, c]]))))
    cols = np.stack(cols)
    return project_t, project, reduce3, rows_fwd, cols, left3, right, left_far


def split(v):
    hi = v.astype(BF)
    return hi, (v - hi.astype(F32)).astype(BF)


def dot(a, b):
    return jnp.dot(a, b, preferred_element_type=F32)


def data_const(hi, lo, c_hi, c_lo):
    return dot(jnp.concatenate([hi, lo, hi], axis=1), jnp.concatenate([c_hi, c_hi, c_lo], axis=0))


def const_data(c_hi, c_lo, hi, lo):
    return dot(jnp.concatenate([c_hi, c_hi, c_lo], axis=1), jnp.concatenate([hi, lo, hi], axis=0))


def soft(v, t):
    return v - jnp.minimum(jnp.maximum(v, -t), t)


def residues(re, im):
    (a_re, b_re, c_re, d_re), (a_im, b_im, c_im, d_im) = (
        (v[0] + v[2], v[1] + v[3], v[0] - v[2], v[1] - v[3]) for v in (re, im)
    )
    return [
        jnp.concatenate(pair, axis=1)
        for pair in (
            (a_re + b_re, a_im + b_im),
            (c_re + d_im, c_im - d_re),
            (a_re - b_re, a_im - b_im),
            (c_re - d_im, c_im + d_re),
        )
    ]


NEAR = [(0, 1), (0, -1)]
FAR = [(1, 0), (-1, 0), (1, 1), (1, -1), (-1, 1), (-1, -1)]


def kernel(
    bands,
    sky,
    ids_ref,
    count_ref,
    weight_ref,
    thr_ref,
    res_in,
    beam_hbm,
    project_t_hbm,
    project_hbm,
    reduce_hbm,
    rows_hbm,
    cols_hbm,
    left_hbm,
    right_hbm,
    left_far_hbm,
    model_out,
    res_out,
    beam,
    project_t,
    project,
    reduce,
    rows_half,
    cols,
    left,
    right,
    left_far,
    rows_fwd,
    rows_inv,
    cols_t,
    gather,
    sky_buf,
    far_out,
    far_in,
    coef3,
    far3,
    own3,
    win,
    spec,
    beam_f,
    const_sem,
    band_send,
    band_recv,
    sky_send,
    sky_recv,
):
    tile = res_in.shape[0]
    half = tile // 2
    levels = left.shape[0]
    slab = tile // bands
    sky_rows = sky // TGX
    me = lax.axis_index("band")
    spot = lax.axis_index("sky")
    row, col = spot // TGX, spot % TGX

    def sky_id(dr, dc):
        return ((row + dr + sky_rows) % sky_rows) * TGX + (col + dc + TGX) % TGX

    pairs = [
        (project_t_hbm, project_t),
        (project_hbm, project),
        (beam_hbm, beam),
        (rows_hbm, rows_half),
        (cols_hbm, cols),
        (reduce_hbm, reduce),
        (left_hbm, left),
        (right_hbm, right),
        (left_far_hbm, left_far),
    ]
    copies = [
        pltpu.make_async_copy(src, dst, const_sem.at[i]) for i, (src, dst) in enumerate(pairs)
    ]
    for copy in copies:
        copy.start()

    barrier = pltpu.get_barrier_semaphore()
    for d in range(1, bands):
        pl.semaphore_signal(
            barrier, inc=1, device_id={"band": (me + d) % bands}, device_id_type=MESH
        )
    for dr, dc in NEAR + FAR:
        pl.semaphore_signal(barrier, inc=1, device_id={"sky": sky_id(dr, dc)}, device_id_type=MESH)

    res_out[...] = res_in[...]
    model_out[...] = jnp.zeros_like(model_out)

    lane = lax.broadcasted_iota(jnp.int32, (1, 128), 1)
    lane16 = lax.broadcasted_iota(jnp.int32, (16, 128), 1)
    flags = []
    for q in range(4):
        live = jnp.float32(0.0)
        for s in range(4):
            hit = jnp.where(ids_ref[s] == q, 1.0, 0.0) * jnp.where(s < count_ref[0], 1.0, 0.0)
            live = live + hit
        flags.append(live)
    weights = [weight_ref[k, me] for k in range(3)]
    scale = jnp.zeros((1, 128), F32)
    for k in range(3):
        ours = (lane >= RANK * k) & (lane < RANK * (k + 1))
        scale = jnp.where(ours, GAIN * weights[k], scale)

    def band_copy(cyc, d):
        return pltpu.make_async_remote_copy(
            src_ref=gather.at[cyc, 0],
            dst_ref=gather.at[cyc, d],
            send_sem=band_send.at[cyc, d],
            recv_sem=band_recv.at[cyc, d],
            device_id={"band": (me + d) % bands},
            device_id_type=MESH,
        )

    def near_slot(dc):
        return (dc + 3) % 3

    def sky_copy(cyc, dr, dc):
        if dr == 0:
            src, dst = sky_buf.at[cyc, 0], sky_buf.at[cyc, near_slot(-dc)]
        else:
            src, dst = far_out.at[cyc, (1 - dr) // 2], far_in.at[cyc, far_slot(-dr, -dc)]
        slot = (1 - dr) * 3 + (1 - dc)
        return pltpu.make_async_remote_copy(
            src_ref=src,
            dst_ref=dst,
            send_sem=sky_send.at[cyc, slot],
            recv_sem=sky_recv.at[cyc, slot],
            device_id={"sky": sky_id(dr, dc)},
            device_id_type=MESH,
        )

    def far_slot(dr, dc):
        return (dr + 1) // 2 * 3 + dc + 1

    def inside(dr, dc):
        return (row + dr >= 0) & (row + dr < sky_rows) & (col + dc >= 0) & (col + dc < TGX)

    for dr, dc in NEAR + FAR:

        @pl.when(jnp.logical_not(inside(dr, dc)))
        def _():
            for cyc in range(CYCLES):
                if dr == 0:
                    sky_buf[cyc, near_slot(dc)] = jnp.zeros((KPAD, 128), F32)
                else:
                    far_in[cyc, far_slot(dr, dc)] = jnp.zeros((FAR_RANK, 128), F32)

    def send(cyc, where):
        for dr, dc in where:

            @pl.when(inside(dr, dc))
            def _():
                sky_copy(cyc, dr, dc).start()

    def receive(cyc, where):
        for dr, dc in where:

            @pl.when(inside(dr, dc))
            def _():
                sky_copy(cyc, -dr, -dc).wait_recv()

    def with_flags(v):
        r = lax.broadcasted_iota(jnp.int32, v.shape, 0)
        c = lax.broadcasted_iota(jnp.int32, v.shape, 1)
        for q in range(4):
            v = jnp.where((c == 127) & (r == q), flags[q], v)
        return v

    def prepare():
        for copy in copies[2:5]:
            copy.wait()
        alt = (1 - 2 * (lax.broadcasted_iota(jnp.int32, (tile, 1), 0) % 2)).astype(F32)
        b_hi, b_lo = split(beam[...])
        first = const_data(rows_half[0], rows_half[1], b_hi, b_lo)
        blank = jnp.zeros((tile, half), F32)
        re, im = (
            [first[at : at + tile, :half], first[at : at + tile, half:], blank, blank]
            for at in (0, tile)
        )
        norm = 2.0 / (4 * tile * tile)
        for r, v in enumerate(residues(re, im)):
            hi, lo = split(v)
            beam_f[r] = norm * data_const(hi, lo, cols[r, 0], cols[r, 1])
        for part in range(2):
            re = rows_half[part, :tile].astype(F32)
            im = rows_half[part, tile:].astype(F32)
            re_far, im_far = im * alt, -(re * alt)
            rows_fwd[part, :, :tile] = rows_half[part]
            rows_fwd[part, :tile, tile:] = re_far.astype(BF)
            rows_fwd[part, tile:, tile:] = im_far.astype(BF)
            rows_inv[part, :, :tile] = re_far.T.astype(BF)
            rows_inv[part, :, tile:] = im_far.T.astype(BF)
            for r in range(4):
                cols_t[r, part] = cols[r, part].astype(F32).T.astype(BF)
        for copy in copies[5:]:
            copy.wait()

    def place(dst, lanes, v):
        hi, lo = split(v * scale)
        dst[:, 128 * lanes : 128 * (lanes + 1)] = jnp.concatenate([hi, lo, hi], axis=0)

    def expand(v):
        lanes = lax.broadcasted_iota(jnp.int32, v.shape, 1)
        hi, lo = split(v)

        def moved(x, by):
            return x if by == 0 else pltpu.roll(x, by % 128, 1)

        out = []
        for k in range(3):
            low = moved(hi, -RANK * k)
            mid = moved(lo, RANK - RANK * k)
            top = moved(hi, 2 * RANK - RANK * k)
            out.append(jnp.where(lanes < RANK, low, jnp.where(lanes < 2 * RANK, mid, top)))
        return out

    def smooth(phase):
        chunk = half // 2
        blank = jnp.zeros((128, half), BF)

        def pack(j, c):
            rows = slice(chunk * c, chunk * (c + 1))
            if phase == 0:
                first = dot(left[j, rows, :], coef3[...])
            else:
                rows = slice(chunk * (c % 2), chunk * (c % 2 + 1))
                first = dot(left_far[j, c // 2, rows, :], far3[c // 2])
            west, mid, east = (expand(first[:, 128 * t : 128 * (t + 1)]) for t in range(3))
            pairs = [jnp.concatenate([west[k], east[k]], axis=1) for k in range(3)]
            return jnp.concatenate(mid, axis=0), jnp.concatenate(pairs, axis=0)

        def add(j, c, mid, pairs):
            rows = slice(chunk * c, chunk * (c + 1))
            table = right[j]
            both = jnp.concatenate(
                [
                    jnp.concatenate([table[:, half:], blank], axis=1),
                    jnp.concatenate([blank, table[:, :half]], axis=1),
                ],
                axis=0,
            )
            for at, got in ((0, dot(mid, table)), (tile, dot(pairs, both))):
                new = None if j == 0 else win[phase, rows, at : at + tile]
                for k in range(3):
                    cut = GAIN * jnp.abs(weights[k]) * thr_ref[j, k]
                    term = soft(got[chunk * k : chunk * (k + 1)], cut)
                    new = term if new is None else new + term
                win[phase, rows, at : at + tile] = new

        def model(j):
            at = pl.multiple_of(me * slab, slab)
            mine = expand(dot(left[j, pl.ds(at, slab), :], own3[...]))
            got = dot(jnp.concatenate(mine, axis=0), right[j])
            for k in range(3):
                term = GAIN * soft(got[slab * k : slab * (k + 1)], thr_ref[j, k])
                model_out[k] += term

        packed = {}
        for step in range(levels + 1):
            for c in range(4):
                if step < levels:
                    packed[step, c] = pack(step, c)
                if step > 0:
                    add(step - 1, c, *packed.pop((step - 1, c)))
            if phase == 0 and step < levels:
                model(step)

    def masked(cyc, phase, bands_of_rows):
        rows = []
        for at, (dr, qr) in enumerate(bands_of_rows):
            blocks = []
            for (dc, qc), src in (((-1, 1), tile), ((0, 0), 0), ((0, 1), half), ((1, 0), tile + half)):
                q = 2 * qr + qc
                if dr == 0:
                    flag = sky_buf[cyc, near_slot(dc), q : q + 1, 127:128]
                else:
                    flag = far_in[cyc, far_slot(dr, dc), q : q + 1, 127:128]
                blocks.append(win[phase, half * at : half * (at + 1), src : src + half] * flag)
            rows.append(jnp.concatenate(blocks, axis=1))
        return split(jnp.concatenate(rows, axis=0))

    def cycle(cyc, carry):
        r_hi, r_lo = split(res_out[...])
        part = dot(project_t[...], jnp.concatenate([r_hi, r_lo, r_hi], axis=0))
        p_hi, p_lo = split(part)
        coef = dot(jnp.concatenate([p_hi, p_lo, p_hi], axis=1), project[...])
        gather[cyc, 0] = (
            coef[0:16] + pltpu.roll(coef[16:32], RANK, 1) + pltpu.roll(coef[32:48], 2 * RANK, 1)
        )

        for d in range(1, bands):
            band_copy(cyc, d).start()

        @pl.when(cyc == 0)
        def _():
            prepare()

        for d in range(1, bands):
            band_copy(cyc, d).wait_recv()
        sums = []
        for k in range(3):
            total = weights[k] * gather[cyc, 0]
            for d in range(1, bands):
                total = total + weight_ref[k, (me - d + bands) % bands] * gather[cyc, d]
            sums.append(total)
        groups = []
        for g in range(3):
            out = jnp.zeros((16, 128), F32)
            for k in range(3):
                moved = sums[k]
                if k != g:
                    moved = pltpu.roll(moved, (RANK * (k - g)) % 128, 1)
                ours = (lane16 >= RANK * k) & (lane16 < RANK * (k + 1))
                out = jnp.where(ours, moved, out)
            groups.append(out)
        full = jnp.concatenate(groups, axis=0)
        o_hi, o_lo = split(full)
        stacked = jnp.concatenate([o_hi, o_lo, o_hi], axis=0)
        less = dot(reduce[...], stacked)
        for i in range(2):
            far_out[cyc, i] = with_flags(less[FAR_RANK * i : FAR_RANK * (i + 1)])
        send(cyc, FAR)
        sky_buf[cyc, 0] = with_flags(full)
        send(cyc, NEAR)
        own3[...] = stacked
        place(coef3, 1, full)
        receive(cyc, NEAR)
        for dr, dc in NEAR:
            place(coef3, dc + 1, sky_buf[cyc, near_slot(dc)])
        smooth(0)
        w_hi, w_lo = masked(cyc, 0, [(0, 0), (0, 1)])
        inner = slice(half, half + tile)
        spec[...] = const_data(rows_fwd[0, :, inner], rows_fwd[1, :, inner], w_hi, w_lo)

        receive(cyc, FAR)
        for dr, dc in FAR:
            place(far3.at[(dr + 1) // 2], dc + 1, far_in[cyc, far_slot(dr, dc)])
        smooth(1)
        w_hi, w_lo = masked(cyc, 1, [(-1, 1), (1, 0)])

        def outer(part):
            return jnp.concatenate(
                [rows_fwd[part, :, :half], rows_fwd[part, :, half + tile :]], axis=1
            )

        full_spec = spec[...] + const_data(outer(0), outer(1), w_hi, w_lo)
        re, im = (
            [full_spec[at : at + tile, half * m : half * (m + 1)] for m in range(4)]
            for at in (0, tile)
        )
        back = []
        for r, v in enumerate(residues(re, im)):
            hi, lo = split(v)
            x = data_const(hi, lo, cols[r, 0], cols[r, 1])
            x_re, x_im = x[:, :half], x[:, half:]
            b_re, b_im = beam_f[r, :, :half], beam_f[r, :, half:]
            hi, lo = split(
                jnp.concatenate([x_re * b_re - x_im * b_im, x_re * b_im + x_im * b_re], axis=1)
            )
            back.append(data_const(hi, lo, cols_t[r, 0], cols_t[r, 1]))
        even, odd = back[0] + back[2], back[1] + back[3]
        gap, turn = back[0] - back[2], back[1] - back[3]
        z_re = jnp.concatenate(
            [even[:, :half] - odd[:, :half], gap[:, :half] + turn[:, half:]], axis=1
        )
        z_im = jnp.concatenate(
            [even[:, half:] - odd[:, half:], gap[:, half:] - turn[:, :half]], axis=1
        )
        z_hi, z_lo = split(jnp.concatenate([z_re, z_im], axis=0))
        res_out[...] = res_out[...] - const_data(rows_inv[0], rows_inv[1], z_hi, z_lo)
        for d in range(1, bands):
            band_copy(cyc, d).wait_send()
        for dr, dc in NEAR + FAR:

            @pl.when(inside(dr, dc))
            def _():
                sky_copy(cyc, dr, dc).wait_send()

        return carry

    copies[0].wait()
    copies[1].wait()
    pl.semaphore_wait(barrier, bands - 1 + 8)
    lax.fori_loop(0, CYCLES, cycle, 0)


def finish(model_in, res_in, model_out, res_out):
    model_out[...] = model_in[...]
    res_out[...] = res_in[...]


def on_device(residual_start, beam_pattern, spec_weights, thresholds, block_ids, block_counts):
    bands = lax.axis_size("band")
    sky = lax.axis_size("sky")
    tile = residual_start.shape[-1]
    coefs = spec_weights.shape[1]
    levels = thresholds.shape[0]
    tables = host_tables(tile, levels)
    smem = pl.BlockSpec(memory_space=pltpu.SMEM)
    vmem = pl.BlockSpec(memory_space=pltpu.VMEM)
    hbm = pl.BlockSpec(memory_space=pl.ANY)
    region = 2 * tile
    shapes = (
        jax.ShapeDtypeStruct((coefs, tile // bands, tile), F32),
        jax.ShapeDtypeStruct((tile, tile), F32),
    )
    model, res = pl.pallas_call(
        functools.partial(kernel, bands, sky),
        out_shape=shapes,
        in_specs=[smem] * 4 + [vmem] + [hbm] * 9,
        out_specs=(vmem, vmem),
        scratch_shapes=[pltpu.VMEM((tile, tile), F32)]
        + [pltpu.VMEM(t.shape, BF) for t in tables]
        + [
            pltpu.VMEM((2, region, region), BF),
            pltpu.VMEM((2, tile, region), BF),
            pltpu.VMEM((4, 2, tile, tile), BF),
            pltpu.VMEM((CYCLES, bands, 16, 128), F32),
            pltpu.VMEM((CYCLES, 3, KPAD, 128), F32),
            pltpu.VMEM((CYCLES, 2, FAR_RANK, 128), F32),
            pltpu.VMEM((CYCLES, 6, FAR_RANK, 128), F32),
            pltpu.VMEM((3 * KPAD, 384), BF),
            pltpu.VMEM((2, 3 * FAR_RANK, 384), BF),
            pltpu.VMEM((3 * KPAD, 128), BF),
            pltpu.VMEM((2, tile, region), F32),
            pltpu.VMEM((region, region), F32),
            pltpu.VMEM((4, tile, tile), F32),
            pltpu.SemaphoreType.DMA((9,)),
            pltpu.SemaphoreType.DMA((CYCLES, bands)),
            pltpu.SemaphoreType.DMA((CYCLES, bands)),
            pltpu.SemaphoreType.DMA((CYCLES, 9)),
            pltpu.SemaphoreType.DMA((CYCLES, 9)),
        ],
        compiler_params=pltpu.CompilerParams(
            collective_id=0, has_side_effects=True, vmem_limit_bytes=32 << 20
        ),
    )(
        block_ids[0, 0],
        block_counts[0],
        spec_weights.T,
        thresholds,
        *[
            pltpu.with_memory_space_constraint(x, pltpu.HBM)
            for x in (
                residual_start[0, 0],
                beam_pattern[0],
                *[jnp.asarray(t) for t in tables],
            )
        ],
    )
    model, res = pl.pallas_call(
        finish,
        out_shape=shapes,
        in_specs=[vmem] * 2,
        out_specs=(vmem, vmem),
        compiler_params=pltpu.CompilerParams(vmem_limit_bytes=4 << 20),
    )(model, res)
    return (model[:, None], res[None, None])


def solution(mesh):
    placed = (
        P("band", "sky", None, None),
        P("band", None, None),
        P(),
        P(),
        P("band", "sky", None),
        P("band", "sky"),
    )
    return jax.shard_map(
        on_device,
        mesh=mesh,
        in_specs=placed,
        out_specs=(P(None, "sky", "band", None), P("band", "sky", None, None)),
        check_vma=False,
    )
```

```python
import functools

import jax
import jax.numpy as jnp
import numpy as np
from jax import lax
from jax.experimental import pallas as pl
from jax.experimental.pallas import tpu as pltpu
from jax.sharding import PartitionSpec as P

CYCLES = 2
TGX = 4
GAIN = 0.25
RANK = 42
KPAD = 48
FAR_RANK = 32
MESH = pl.DeviceIdType.MESH
BF = jnp.bfloat16
F32 = jnp.float32


def host_split(a):
    hi = np.asarray(a, np.float64).astype(BF)
    lo = (np.asarray(a, np.float64) - hi.astype(np.float64)).astype(BF)
    return hi, lo


def host_tables(tile, levels):
    pos = np.arange(tile, dtype=np.float64)
    off = pos[:, None] - pos[None, :]
    smooth = []
    for j in range(levels):
        spread = 2.0**j * tile / 16.0
        k = np.exp(-off * off / (2.0 * spread * spread))
        smooth.append(k / np.sqrt(np.sum(k * k, axis=1, keepdims=True)))
    smooth = np.stack(smooth)
    _, _, vt = np.linalg.svd(smooth.reshape(-1, tile), full_matrices=False)
    basis = vt[:RANK].T
    proj = np.zeros((tile, 128))
    proj[:, :RANK] = basis
    proj_t = np.zeros((KPAD, tile))
    proj_t[:RANK] = basis.T
    expand = smooth @ basis

    p_hi, p_lo = host_split(proj)
    t_hi, t_lo = host_split(proj_t)
    project = np.concatenate([p_hi, p_hi, p_lo], axis=0)
    project_t = np.concatenate([t_hi, t_hi, t_lo], axis=1)

    left = np.zeros((levels, tile, KPAD))
    left[:, :, :RANK] = expand
    l_hi, l_lo = host_split(left)
    left3 = np.concatenate([l_hi, l_hi, l_lo], axis=2)

    far, reduce = [], np.zeros((2 * FAR_RANK, KPAD))
    for i, rows in enumerate((slice(tile // 2, tile), slice(0, tile // 2))):
        _, _, vt = np.linalg.svd(expand[:, rows].reshape(-1, RANK), full_matrices=False)
        reduce[FAR_RANK * i : FAR_RANK * (i + 1), :RANK] = vt[:FAR_RANK]
        f_hi, f_lo = host_split(expand[:, rows] @ vt[:FAR_RANK].T)
        far.append(np.concatenate([f_hi, f_hi, f_lo], axis=2))
    left_far = np.stack(far, axis=1)
    z_hi, z_lo = host_split(reduce)
    reduce3 = np.concatenate([z_hi, z_hi, z_lo], axis=1)

    right = np.zeros((levels, 128, tile), BF)
    g_hi, g_lo = host_split(expand.transpose(0, 2, 1))
    for p, g in enumerate((g_hi, g_hi, g_lo)):
        right[:, RANK * p : RANK * (p + 1)] = g

    n = 2 * tile
    f = np.arange(tile) + 0.5
    ang = 2.0 * np.pi * f[:, None] * np.arange(tile)[None, :] / n
    rows_fwd = np.stack(host_split(np.concatenate([np.cos(ang), -np.sin(ang)], axis=0)))

    cols = []
    x = np.arange(tile // 2)
    for r in range(4):
        a = 2.0 * np.pi * x[:, None] * (4 * x[None, :] + r) / n
        c, s = np.cos(a), np.sin(a)
        cols.append(np.stack(host_split(np.block([[c, -s], [s, c]]))))
    cols = np.stack(cols)
    return project_t, project, reduce3, rows_fwd, cols, left3, right, left_far


def split(v):
    hi = v.astype(BF)
    return hi, (v - hi.astype(F32)).astype(BF)


def dot(a, b):
    return jnp.dot(a, b, preferred_element_type=F32)


def data_const(hi, lo, c_hi, c_lo):
    return dot(jnp.concatenate([hi, lo, hi], axis=1), jnp.concatenate([c_hi, c_hi, c_lo], axis=0))


def const_data(c_hi, c_lo, hi, lo):
    return dot(jnp.concatenate([c_hi, c_hi, c_lo], axis=1), jnp.concatenate([hi, lo, hi], axis=0))


def soft(v, t):
    return v - jnp.minimum(jnp.maximum(v, -t), t)


def residues(re, im):
    (a_re, b_re, c_re, d_re), (a_im, b_im, c_im, d_im) = (
        (v[0] + v[2], v[1] + v[3], v[0] - v[2], v[1] - v[3]) for v in (re, im)
    )
    return [
        jnp.concatenate(pair, axis=1)
        for pair in (
            (a_re + b_re, a_im + b_im),
            (c_re + d_im, c_im - d_re),
            (a_re - b_re, a_im - b_im),
            (c_re - d_im, c_im + d_re),
        )
    ]


NEAR = [(0, 1), (0, -1)]
FAR = [(1, 0), (-1, 0), (1, 1), (1, -1), (-1, 1), (-1, -1)]


def kernel(
    bands,
    sky,
    ids_hbm,
    count_hbm,
    weight_hbm,
    thr_hbm,
    res_hbm,
    beam_hbm,
    project_t_hbm,
    project_hbm,
    reduce_hbm,
    rows_hbm,
    cols_hbm,
    left_hbm,
    right_hbm,
    left_far_hbm,
    model_out,
    res_out,
    ids_ref,
    count_ref,
    weight_ref,
    thr_ref,
    beam,
    project_t,
    project,
    reduce,
    rows_half,
    cols,
    left,
    right,
    left_far,
    rows_fwd,
    rows_inv,
    cols_t,
    gather,
    sky_buf,
    far_out,
    far_in,
    coef3,
    far3,
    own3,
    win,
    spec,
    beam_f,
    const_sem,
    band_send,
    band_recv,
    sky_send,
    sky_recv,
):
    tile = res_out.shape[0]
    half = tile // 2
    levels = left.shape[0]
    slab = tile // bands
    sky_rows = sky // TGX
    me = lax.axis_index("band")
    spot = lax.axis_index("sky")
    row, col = spot // TGX, spot % TGX

    def sky_id(dr, dc):
        return ((row + dr + sky_rows) % sky_rows) * TGX + (col + dc + TGX) % TGX

    pairs = [
        (res_hbm, res_out),
        (project_t_hbm, project_t),
        (project_hbm, project),
        (beam_hbm, beam),
        (rows_hbm, rows_half),
        (cols_hbm, cols),
        (reduce_hbm, reduce),
        (left_hbm, left),
        (right_hbm, right),
        (left_far_hbm, left_far),
        (ids_hbm, ids_ref),
        (count_hbm, count_ref),
        (weight_hbm, weight_ref),
        (thr_hbm, thr_ref),
    ]
    copies = [
        pltpu.make_async_copy(src, dst, const_sem.at[i]) for i, (src, dst) in enumerate(pairs)
    ]
    for copy in copies[:3]:
        copy.start()

    barrier = pltpu.get_barrier_semaphore()
    for d in range(1, bands):
        pl.semaphore_signal(
            barrier, inc=1, device_id={"band": (me + d) % bands}, device_id_type=MESH
        )
    for dr, dc in NEAR + FAR:
        pl.semaphore_signal(barrier, inc=1, device_id={"sky": sky_id(dr, dc)}, device_id_type=MESH)

    for copy in copies[3:]:
        copy.start()

    def band_copy(cyc, d):
        return pltpu.make_async_remote_copy(
            src_ref=gather.at[cyc, 0],
            dst_ref=gather.at[cyc, d],
            send_sem=band_send.at[cyc, d],
            recv_sem=band_recv.at[cyc, d],
            device_id={"band": (me + d) % bands},
            device_id_type=MESH,
        )

    def compress(cyc):
        r_hi, r_lo = split(res_out[...])
        part = dot(project_t[...], jnp.concatenate([r_hi, r_lo, r_hi], axis=0))
        p_hi, p_lo = split(part)
        coef = dot(jnp.concatenate([p_hi, p_lo, p_hi], axis=1), project[...])
        gather[cyc, 0] = (
            coef[0:16] + pltpu.roll(coef[16:32], RANK, 1) + pltpu.roll(coef[32:48], 2 * RANK, 1)
        )
        if isinstance(cyc, int):
            pl.semaphore_wait(barrier, bands - 1 + 8)
        for d in range(1, bands):
            band_copy(cyc, d).start()

    for copy in copies[:3]:
        copy.wait()
    compress(0)

    model_out[...] = jnp.zeros_like(model_out)

    lane = lax.broadcasted_iota(jnp.int32, (1, 128), 1)
    lane16 = lax.broadcasted_iota(jnp.int32, (16, 128), 1)
    for copy in copies[10:]:
        copy.wait()
    flags = []
    for q in range(4):
        live = jnp.float32(0.0)
        for s in range(4):
            hit = jnp.where(ids_ref[s] == q, 1.0, 0.0) * jnp.where(s < count_ref[0], 1.0, 0.0)
            live = live + hit
        flags.append(live)
    weights = [weight_ref[k, me] for k in range(3)]
    scale = jnp.zeros((1, 128), F32)
    for k in range(3):
        ours = (lane >= RANK * k) & (lane < RANK * (k + 1))
        scale = jnp.where(ours, GAIN * weights[k], scale)

    def near_slot(dc):
        return (dc + 3) % 3

    def sky_copy(cyc, dr, dc):
        if dr == 0:
            src, dst = sky_buf.at[cyc, 0], sky_buf.at[cyc, near_slot(-dc)]
        else:
            src, dst = far_out.at[cyc, (1 - dr) // 2], far_in.at[cyc, far_slot(-dr, -dc)]
        slot = (1 - dr) * 3 + (1 - dc)
        return pltpu.make_async_remote_copy(
            src_ref=src,
            dst_ref=dst,
            send_sem=sky_send.at[cyc, slot],
            recv_sem=sky_recv.at[cyc, slot],
            device_id={"sky": sky_id(dr, dc)},
            device_id_type=MESH,
        )

    def far_slot(dr, dc):
        return (dr + 1) // 2 * 3 + dc + 1

    def inside(dr, dc):
        return (row + dr >= 0) & (row + dr < sky_rows) & (col + dc >= 0) & (col + dc < TGX)

    for dr, dc in NEAR + FAR:

        @pl.when(jnp.logical_not(inside(dr, dc)))
        def _():
            for cyc in range(CYCLES):
                if dr == 0:
                    sky_buf[cyc, near_slot(dc)] = jnp.zeros((KPAD, 128), F32)
                else:
                    far_in[cyc, far_slot(dr, dc)] = jnp.zeros((FAR_RANK, 128), F32)

    def send(cyc, where):
        for dr, dc in where:

            @pl.when(inside(dr, dc))
            def _():
                sky_copy(cyc, dr, dc).start()

    def receive(cyc, where):
        for dr, dc in where:

            @pl.when(inside(dr, dc))
            def _():
                sky_copy(cyc, -dr, -dc).wait_recv()

    def with_flags(v):
        r = lax.broadcasted_iota(jnp.int32, v.shape, 0)
        c = lax.broadcasted_iota(jnp.int32, v.shape, 1)
        for q in range(4):
            v = jnp.where((c == 127) & (r == q), flags[q], v)
        return v

    def prepare():
        for copy in copies[3:6]:
            copy.wait()
        alt = (1 - 2 * (lax.broadcasted_iota(jnp.int32, (tile, 1), 0) % 2)).astype(F32)
        b_hi, b_lo = split(beam[...])
        first = const_data(rows_half[0], rows_half[1], b_hi, b_lo)
        blank = jnp.zeros((tile, half), F32)
        re, im = (
            [first[at : at + tile, :half], first[at : at + tile, half:], blank, blank]
            for at in (0, tile)
        )
        norm = 2.0 / (4 * tile * tile)
        for r, v in enumerate(residues(re, im)):
            hi, lo = split(v)
            beam_f[r] = norm * data_const(hi, lo, cols[r, 0], cols[r, 1])
        for part in range(2):
            re = rows_half[part, :tile].astype(F32)
            im = rows_half[part, tile:].astype(F32)
            re_far, im_far = im * alt, -(re * alt)
            rows_fwd[part, :, :tile] = rows_half[part]
            rows_fwd[part, :tile, tile:] = re_far.astype(BF)
            rows_fwd[part, tile:, tile:] = im_far.astype(BF)
            rows_inv[part, :, :tile] = re_far.T.astype(BF)
            rows_inv[part, :, tile:] = im_far.T.astype(BF)
            for r in range(4):
                cols_t[r, part] = cols[r, part].astype(F32).T.astype(BF)
        for copy in copies[6:10]:
            copy.wait()

    prepare()

    def place(dst, lanes, v):
        hi, lo = split(v * scale)
        dst[:, 128 * lanes : 128 * (lanes + 1)] = jnp.concatenate([hi, lo, hi], axis=0)

    def expand(v):
        lanes = lax.broadcasted_iota(jnp.int32, v.shape, 1)
        hi, lo = split(v)

        def moved(x, by):
            return x if by == 0 else pltpu.roll(x, by % 128, 1)

        out = []
        for k in range(3):
            low = moved(hi, -RANK * k)
            mid = moved(lo, RANK - RANK * k)
            top = moved(hi, 2 * RANK - RANK * k)
            out.append(jnp.where(lanes < RANK, low, jnp.where(lanes < 2 * RANK, mid, top)))
        return out

    def smooth(phase):
        chunk = half // 2
        blank = jnp.zeros((128, half), BF)

        def pack(j, c):
            rows = slice(chunk * c, chunk * (c + 1))
            if phase == 0:
                first = dot(left[j, rows, :], coef3[...])
            else:
                rows = slice(chunk * (c % 2), chunk * (c % 2 + 1))
                first = dot(left_far[j, c // 2, rows, :], far3[c // 2])
            west, mid, east = (expand(first[:, 128 * t : 128 * (t + 1)]) for t in range(3))
            pairs = [jnp.concatenate([west[k], east[k]], axis=1) for k in range(3)]
            return jnp.concatenate(mid, axis=0), jnp.concatenate(pairs, axis=0)

        def add(j, c, mid, pairs):
            rows = slice(chunk * c, chunk * (c + 1))
            table = right[j]
            both = jnp.concatenate(
                [
                    jnp.concatenate([table[:, half:], blank], axis=1),
                    jnp.concatenate([blank, table[:, :half]], axis=1),
                ],
                axis=0,
            )
            for at, got in ((0, dot(mid, table)), (tile, dot(pairs, both))):
                new = None if j == 0 else win[phase, rows, at : at + tile]
                for k in range(3):
                    cut = GAIN * jnp.abs(weights[k]) * thr_ref[j, k]
                    term = soft(got[chunk * k : chunk * (k + 1)], cut)
                    new = term if new is None else new + term
                win[phase, rows, at : at + tile] = new

        def model(j):
            at = pl.multiple_of(me * slab, slab)
            mine = expand(dot(left[j, pl.ds(at, slab), :], own3[...]))
            got = dot(jnp.concatenate(mine, axis=0), right[j])
            for k in range(3):
                term = GAIN * soft(got[slab * k : slab * (k + 1)], thr_ref[j, k])
                model_out[k] += term

        packed = {}
        for step in range(levels + 1):
            for c in range(4):
                if step < levels:
                    packed[step, c] = pack(step, c)
                if step > 0:
                    add(step - 1, c, *packed.pop((step - 1, c)))
            if phase == 0 and step < levels:
                model(step)

    def masked(cyc, phase, bands_of_rows):
        rows = []
        for at, (dr, qr) in enumerate(bands_of_rows):
            blocks = []
            for (dc, qc), src in (((-1, 1), tile), ((0, 0), 0), ((0, 1), half), ((1, 0), tile + half)):
                q = 2 * qr + qc
                if dr == 0:
                    flag = sky_buf[cyc, near_slot(dc), q : q + 1, 127:128]
                else:
                    flag = far_in[cyc, far_slot(dr, dc), q : q + 1, 127:128]
                blocks.append(win[phase, half * at : half * (at + 1), src : src + half] * flag)
            rows.append(jnp.concatenate(blocks, axis=1))
        return split(jnp.concatenate(rows, axis=0))

    def cycle(cyc, carry):
        for d in range(1, bands):
            band_copy(cyc, d).wait_recv()
        sums = []
        for k in range(3):
            total = weights[k] * gather[cyc, 0]
            for d in range(1, bands):
                total = total + weight_ref[k, (me - d + bands) % bands] * gather[cyc, d]
            sums.append(total)
        groups = []
        for g in range(3):
            out = jnp.zeros((16, 128), F32)
            for k in range(3):
                moved = sums[k]
                if k != g:
                    moved = pltpu.roll(moved, (RANK * (k - g)) % 128, 1)
                ours = (lane16 >= RANK * k) & (lane16 < RANK * (k + 1))
                out = jnp.where(ours, moved, out)
            groups.append(out)
        full = jnp.concatenate(groups, axis=0)
        o_hi, o_lo = split(full)
        stacked = jnp.concatenate([o_hi, o_lo, o_hi], axis=0)
        less = dot(reduce[...], stacked)
        for i in range(2):
            far_out[cyc, i] = with_flags(less[FAR_RANK * i : FAR_RANK * (i + 1)])
        send(cyc, FAR)
        sky_buf[cyc, 0] = with_flags(full)
        send(cyc, NEAR)
        own3[...] = stacked
        place(coef3, 1, full)
        receive(cyc, NEAR)
        for dr, dc in NEAR:
            place(coef3, dc + 1, sky_buf[cyc, near_slot(dc)])
        smooth(0)
        w_hi, w_lo = masked(cyc, 0, [(0, 0), (0, 1)])
        inner = slice(half, half + tile)
        spec[...] = const_data(rows_fwd[0, :, inner], rows_fwd[1, :, inner], w_hi, w_lo)

        receive(cyc, FAR)
        for dr, dc in FAR:
            place(far3.at[(dr + 1) // 2], dc + 1, far_in[cyc, far_slot(dr, dc)])
        smooth(1)
        w_hi, w_lo = masked(cyc, 1, [(-1, 1), (1, 0)])

        w_rows = jnp.concatenate([w_hi, w_lo, w_hi], axis=0)
        part_rows = half

        def freqs(c):
            return [slice(at + part_rows * c, at + part_rows * (c + 1)) for at in (0, tile)]

        def start(c):
            def outer(part):
                return jnp.concatenate(
                    [
                        jnp.concatenate(
                            [rows_fwd[part, f, :half], rows_fwd[part, f, half + tile :]], axis=1
                        )
                        for f in freqs(c)
                    ],
                    axis=0,
                )

            hi = outer(0)
            got = dot(jnp.concatenate([hi, hi, outer(1)], axis=1), w_rows)
            re, im = (
                got[part_rows * i : part_rows * (i + 1)] + spec[f, :]
                for i, f in enumerate(freqs(c))
            )
            blocks = [[v[:, half * m : half * (m + 1)] for m in range(4)] for v in (re, im)]
            return [split(v) for v in residues(*blocks)]

        def along(pair, r):
            return data_const(*pair, cols[r, 0], cols[r, 1])

        def back(r, x):
            x_re, x_im = x[:, :half], x[:, half:]
            b_re, b_im = beam_f[r, :, :half], beam_f[r, :, half:]
            hi, lo = split(
                jnp.concatenate([x_re * b_re - x_im * b_im, x_re * b_im + x_im * b_re], axis=1)
            )
            return data_const(hi, lo, cols_t[r, 0], cols_t[r, 1])

        first, second = start(0), start(1)
        x, t = [], []
        for r in range(4):
            pair = [jnp.concatenate([first[r][i], second[r][i]], axis=0) for i in range(2)]
            x.append(along(pair, r))
            if r > 0:
                t.append(back(r - 1, x[r - 1]))
        t.append(back(3, x[3]))
        even, odd, gap, turn = t[0] + t[2], t[1] + t[3], t[0] - t[2], t[1] - t[3]
        z_re = jnp.concatenate(
            [even[:, :half] - odd[:, :half], gap[:, :half] + turn[:, half:]], axis=1
        )
        z_im = jnp.concatenate(
            [even[:, half:] - odd[:, half:], gap[:, half:] - turn[:, :half]], axis=1
        )
        z_hi, z_lo = split(jnp.concatenate([z_re, z_im], axis=0))
        res_out[...] = res_out[...] - const_data(rows_inv[0], rows_inv[1], z_hi, z_lo)

        @pl.when(cyc + 1 < CYCLES)
        def _():
            compress(cyc + 1)

        return carry

    lax.fori_loop(0, CYCLES, cycle, 0)
    for cyc in range(CYCLES):
        for d in range(1, bands):
            band_copy(cyc, d).wait_send()
        for dr, dc in NEAR + FAR:

            @pl.when(inside(dr, dc))
            def _():
                sky_copy(cyc, dr, dc).wait_send()


def finish(model_in, res_in, model_out, res_out):
    model_out[...] = model_in[...]
    res_out[...] = res_in[...]


def on_device(residual_start, beam_pattern, spec_weights, thresholds, block_ids, block_counts):
    bands = lax.axis_size("band")
    sky = lax.axis_size("sky")
    tile = residual_start.shape[-1]
    coefs = spec_weights.shape[1]
    levels = thresholds.shape[0]
    tables = host_tables(tile, levels)
    vmem = pl.BlockSpec(memory_space=pltpu.VMEM)
    hbm = pl.BlockSpec(memory_space=pl.ANY)
    region = 2 * tile
    shapes = (
        jax.ShapeDtypeStruct((coefs, tile // bands, tile), F32),
        jax.ShapeDtypeStruct((tile, tile), F32),
    )
    model, res = pl.pallas_call(
        functools.partial(kernel, bands, sky),
        out_shape=shapes,
        in_specs=[hbm] * 14,
        out_specs=(vmem, vmem),
        scratch_shapes=[
            pltpu.SMEM((4,), jnp.int32),
            pltpu.SMEM((1,), jnp.int32),
            pltpu.SMEM((coefs, bands), F32),
            pltpu.SMEM((levels, coefs), F32),
            pltpu.VMEM((tile, tile), F32),
        ]
        + [pltpu.VMEM(t.shape, BF) for t in tables]
        + [
            pltpu.VMEM((2, region, region), BF),
            pltpu.VMEM((2, tile, region), BF),
            pltpu.VMEM((4, 2, tile, tile), BF),
            pltpu.VMEM((CYCLES, bands, 16, 128), F32),
            pltpu.VMEM((CYCLES, 3, KPAD, 128), F32),
            pltpu.VMEM((CYCLES, 2, FAR_RANK, 128), F32),
            pltpu.VMEM((CYCLES, 6, FAR_RANK, 128), F32),
            pltpu.VMEM((3 * KPAD, 384), BF),
            pltpu.VMEM((2, 3 * FAR_RANK, 384), BF),
            pltpu.VMEM((3 * KPAD, 128), BF),
            pltpu.VMEM((2, tile, region), F32),
            pltpu.VMEM((region, region), F32),
            pltpu.VMEM((4, tile, tile), F32),
            pltpu.SemaphoreType.DMA((14,)),
            pltpu.SemaphoreType.DMA((CYCLES, bands)),
            pltpu.SemaphoreType.DMA((CYCLES, bands)),
            pltpu.SemaphoreType.DMA((CYCLES, 9)),
            pltpu.SemaphoreType.DMA((CYCLES, 9)),
        ],
        compiler_params=pltpu.CompilerParams(
            collective_id=0, has_side_effects=True, vmem_limit_bytes=32 << 20
        ),
    )(
        pltpu.with_memory_space_constraint(block_ids[0, 0], pltpu.HBM),
        block_counts[0],
        *[
            pltpu.with_memory_space_constraint(x, pltpu.HBM)
            for x in (
                spec_weights.T,
                thresholds,
                residual_start[0, 0],
                beam_pattern[0],
                *[jnp.asarray(t) for t in tables],
            )
        ],
    )
    model, res = pl.pallas_call(
        finish,
        out_shape=shapes,
        in_specs=[vmem] * 2,
        out_specs=(vmem, vmem),
        compiler_params=pltpu.CompilerParams(vmem_limit_bytes=4 << 20),
    )(model, res)
    return (model[:, None], res[None, None])


def solution(mesh):
    placed = (
        P("band", "sky", None, None),
        P("band", None, None),
        P(),
        P(),
        P("band", "sky", None),
        P("band", "sky"),
    )
    return jax.shard_map(
        on_device,
        mesh=mesh,
        in_specs=placed,
        out_specs=(P(None, "sky", "band", None), P("band", "sky", None, None)),
        check_vma=False,
    )
```

```python
import functools

import jax
import jax.numpy as jnp
import numpy as np
from jax import lax
from jax.experimental import pallas as pl
from jax.experimental.pallas import tpu as pltpu
from jax.sharding import PartitionSpec as P

CYCLES = 2
TGX = 4
GAIN = 0.25
RANK = 42
KPAD = 48
FAR_RANK = 32
MESH = pl.DeviceIdType.MESH
BF = jnp.bfloat16
F32 = jnp.float32


def host_split(a):
    hi = np.asarray(a, np.float64).astype(BF)
    lo = (np.asarray(a, np.float64) - hi.astype(np.float64)).astype(BF)
    return hi, lo


def host_tables(tile, levels):
    pos = np.arange(tile, dtype=np.float64)
    off = pos[:, None] - pos[None, :]
    smooth = []
    for j in range(levels):
        spread = 2.0**j * tile / 16.0
        k = np.exp(-off * off / (2.0 * spread * spread))
        smooth.append(k / np.sqrt(np.sum(k * k, axis=1, keepdims=True)))
    smooth = np.stack(smooth)
    _, _, vt = np.linalg.svd(smooth.reshape(-1, tile), full_matrices=False)
    basis = vt[:RANK].T
    proj = np.zeros((tile, 128))
    proj[:, :RANK] = basis
    proj_t = np.zeros((KPAD, tile))
    proj_t[:RANK] = basis.T
    expand = smooth @ basis

    p_hi, p_lo = host_split(proj)
    t_hi, t_lo = host_split(proj_t)
    project = np.concatenate([p_hi, p_hi, p_lo], axis=0)
    project_t = np.concatenate([t_hi, t_hi, t_lo], axis=1)

    left = np.zeros((levels, tile, KPAD))
    left[:, :, :RANK] = expand
    l_hi, l_lo = host_split(left)
    left3 = np.concatenate([l_hi, l_hi, l_lo], axis=2)

    far, reduce = [], np.zeros((2 * FAR_RANK, KPAD))
    for i, rows in enumerate((slice(tile // 2, tile), slice(0, tile // 2))):
        _, _, vt = np.linalg.svd(expand[:, rows].reshape(-1, RANK), full_matrices=False)
        reduce[FAR_RANK * i : FAR_RANK * (i + 1), :RANK] = vt[:FAR_RANK]
        f_hi, f_lo = host_split(expand[:, rows] @ vt[:FAR_RANK].T)
        far.append(np.concatenate([f_hi, f_hi, f_lo], axis=2))
    left_far = np.stack(far, axis=1)
    z_hi, z_lo = host_split(reduce)
    reduce3 = np.concatenate([z_hi, z_hi, z_lo], axis=1)

    right = np.zeros((levels, 128, tile), BF)
    g_hi, g_lo = host_split(expand.transpose(0, 2, 1))
    for p, g in enumerate((g_hi, g_hi, g_lo)):
        right[:, RANK * p : RANK * (p + 1)] = g

    n = 2 * tile
    f = np.arange(tile) + 0.5
    ang = 2.0 * np.pi * f[:, None] * np.arange(tile)[None, :] / n
    rows_fwd = np.stack(host_split(np.concatenate([np.cos(ang), -np.sin(ang)], axis=0)))

    cols = []
    x = np.arange(tile // 2)
    for r in range(4):
        a = 2.0 * np.pi * x[:, None] * (4 * x[None, :] + r) / n
        c, s = np.cos(a), np.sin(a)
        cols.append(np.stack(host_split(np.block([[c, -s], [s, c]]))))
    cols = np.stack(cols)
    return project_t, project, reduce3, rows_fwd, cols, left3, right, left_far


def split(v):
    hi = v.astype(BF)
    return hi, (v - hi.astype(F32)).astype(BF)


def dot(a, b):
    return jnp.dot(a, b, preferred_element_type=F32)


def data_const(hi, lo, c_hi, c_lo):
    return dot(jnp.concatenate([hi, lo, hi], axis=1), jnp.concatenate([c_hi, c_hi, c_lo], axis=0))


def const_data(c_hi, c_lo, hi, lo):
    return dot(jnp.concatenate([c_hi, c_hi, c_lo], axis=1), jnp.concatenate([hi, lo, hi], axis=0))


def soft(v, t):
    return v - jnp.minimum(jnp.maximum(v, -t), t)


def residues(re, im):
    (a_re, b_re, c_re, d_re), (a_im, b_im, c_im, d_im) = (
        (v[0] + v[2], v[1] + v[3], v[0] - v[2], v[1] - v[3]) for v in (re, im)
    )
    return [
        jnp.concatenate(pair, axis=1)
        for pair in (
            (a_re + b_re, a_im + b_im),
            (c_re + d_im, c_im - d_re),
            (a_re - b_re, a_im - b_im),
            (c_re - d_im, c_im + d_re),
        )
    ]


NEAR = [(0, 1), (0, -1)]
FAR = [(1, 0), (1, 1), (1, -1), (-1, 0), (-1, 1), (-1, -1)]


def kernel(
    bands,
    sky,
    ids_hbm,
    count_hbm,
    weight_hbm,
    thr_hbm,
    res_hbm,
    beam_hbm,
    project_t_hbm,
    project_hbm,
    reduce_hbm,
    rows_hbm,
    cols_hbm,
    left_hbm,
    right_hbm,
    left_far_hbm,
    model_out,
    res_out,
    ids_ref,
    count_ref,
    weight_ref,
    thr_ref,
    beam,
    project_t,
    project,
    reduce,
    rows_half,
    cols,
    left,
    right,
    left_far,
    rows_fwd,
    rows_inv,
    cols_t,
    gather,
    sky_buf,
    far_out,
    far_in,
    coef3,
    far3,
    own3,
    win,
    spec,
    beam_f,
    const_sem,
    band_send,
    band_recv,
    sky_send,
    sky_recv,
):
    tile = res_out.shape[0]
    half = tile // 2
    levels = left.shape[0]
    slab = tile // bands
    sky_rows = sky // TGX
    me = lax.axis_index("band")
    spot = lax.axis_index("sky")
    row, col = spot // TGX, spot % TGX

    def sky_id(dr, dc):
        return ((row + dr + sky_rows) % sky_rows) * TGX + (col + dc + TGX) % TGX

    pairs = [
        (res_hbm, res_out),
        (project_t_hbm, project_t),
        (project_hbm, project),
        (beam_hbm, beam),
        (rows_hbm, rows_half),
        (cols_hbm, cols),
        (reduce_hbm, reduce),
        (left_hbm, left),
        (right_hbm, right),
        (left_far_hbm, left_far),
        (ids_hbm, ids_ref),
        (count_hbm, count_ref),
        (weight_hbm, weight_ref),
        (thr_hbm, thr_ref),
    ]
    copies = [
        pltpu.make_async_copy(src, dst, const_sem.at[i]) for i, (src, dst) in enumerate(pairs)
    ]
    for copy in copies[:3]:
        copy.start()

    barrier = pltpu.get_barrier_semaphore()
    for d in range(1, bands):
        pl.semaphore_signal(
            barrier, inc=1, device_id={"band": (me + d) % bands}, device_id_type=MESH
        )
    for dr, dc in NEAR + FAR:
        pl.semaphore_signal(barrier, inc=1, device_id={"sky": sky_id(dr, dc)}, device_id_type=MESH)

    for copy in copies[3:]:
        copy.start()

    def band_copy(cyc, d):
        return pltpu.make_async_remote_copy(
            src_ref=gather.at[cyc, 0],
            dst_ref=gather.at[cyc, d],
            send_sem=band_send.at[cyc, d],
            recv_sem=band_recv.at[cyc, d],
            device_id={"band": (me + d) % bands},
            device_id_type=MESH,
        )

    def compress(cyc):
        r_hi, r_lo = split(res_out[...])
        part = dot(project_t[...], jnp.concatenate([r_hi, r_lo, r_hi], axis=0))
        p_hi, p_lo = split(part)
        coef = dot(jnp.concatenate([p_hi, p_lo, p_hi], axis=1), project[...])
        gather[cyc, 0] = (
            coef[0:16] + pltpu.roll(coef[16:32], RANK, 1) + pltpu.roll(coef[32:48], 2 * RANK, 1)
        )
        if isinstance(cyc, int):
            pl.semaphore_wait(barrier, bands - 1 + 8)
        for d in sorted(range(1, bands), key=lambda d: -min(d // 2, (bands - d) // 2)):
            band_copy(cyc, d).start()

    for copy in copies[:3]:
        copy.wait()
    compress(0)

    model_out[...] = jnp.zeros_like(model_out)

    lane = lax.broadcasted_iota(jnp.int32, (1, 128), 1)
    lane16 = lax.broadcasted_iota(jnp.int32, (16, 128), 1)
    for copy in copies[10:]:
        copy.wait()
    flags = []
    for q in range(4):
        live = jnp.float32(0.0)
        for s in range(4):
            hit = jnp.where(ids_ref[s] == q, 1.0, 0.0) * jnp.where(s < count_ref[0], 1.0, 0.0)
            live = live + hit
        flags.append(live)
    weights = [weight_ref[k, me] for k in range(3)]
    scale = jnp.zeros((1, 128), F32)
    for k in range(3):
        ours = (lane >= RANK * k) & (lane < RANK * (k + 1))
        scale = jnp.where(ours, GAIN * weights[k], scale)

    def near_slot(dc):
        return (dc + 3) % 3

    def sky_copy(cyc, dr, dc):
        if dr == 0:
            src, dst = sky_buf.at[cyc, 0], sky_buf.at[cyc, near_slot(-dc)]
        else:
            src, dst = far_out.at[cyc, (1 - dr) // 2], far_in.at[cyc, far_slot(-dr, -dc)]
        slot = (1 - dr) * 3 + (1 - dc)
        return pltpu.make_async_remote_copy(
            src_ref=src,
            dst_ref=dst,
            send_sem=sky_send.at[cyc, slot],
            recv_sem=sky_recv.at[cyc, slot],
            device_id={"sky": sky_id(dr, dc)},
            device_id_type=MESH,
        )

    def far_slot(dr, dc):
        return (dr + 1) // 2 * 3 + dc + 1

    def inside(dr, dc):
        return (row + dr >= 0) & (row + dr < sky_rows) & (col + dc >= 0) & (col + dc < TGX)

    for dr, dc in NEAR + FAR:

        @pl.when(jnp.logical_not(inside(dr, dc)))
        def _():
            for cyc in range(CYCLES):
                if dr == 0:
                    sky_buf[cyc, near_slot(dc)] = jnp.zeros((KPAD, 128), F32)
                else:
                    far_in[cyc, far_slot(dr, dc)] = jnp.zeros((FAR_RANK, 128), F32)

    def send(cyc, where):
        for dr, dc in where:

            @pl.when(inside(dr, dc))
            def _():
                sky_copy(cyc, dr, dc).start()

    def receive(cyc, where):
        for dr, dc in where:

            @pl.when(inside(dr, dc))
            def _():
                sky_copy(cyc, -dr, -dc).wait_recv()

    def with_flags(v):
        r = lax.broadcasted_iota(jnp.int32, v.shape, 0)
        c = lax.broadcasted_iota(jnp.int32, v.shape, 1)
        for q in range(4):
            v = jnp.where((c == 127) & (r == q), flags[q], v)
        return v

    def prepare():
        for copy in copies[3:6]:
            copy.wait()
        alt = (1 - 2 * (lax.broadcasted_iota(jnp.int32, (tile, 1), 0) % 2)).astype(F32)
        b_hi, b_lo = split(beam[...])
        first = const_data(rows_half[0], rows_half[1], b_hi, b_lo)
        blank = jnp.zeros((tile, half), F32)
        re, im = (
            [first[at : at + tile, :half], first[at : at + tile, half:], blank, blank]
            for at in (0, tile)
        )
        norm = 2.0 / (4 * tile * tile)
        for r, v in enumerate(residues(re, im)):
            hi, lo = split(v)
            beam_f[r] = norm * data_const(hi, lo, cols[r, 0], cols[r, 1])
        for part in range(2):
            re = rows_half[part, :tile].astype(F32)
            im = rows_half[part, tile:].astype(F32)
            re_far, im_far = im * alt, -(re * alt)
            rows_fwd[part, :, :tile] = rows_half[part]
            rows_fwd[part, :tile, tile:] = re_far.astype(BF)
            rows_fwd[part, tile:, tile:] = im_far.astype(BF)
            rows_inv[part, :, :tile] = re_far.T.astype(BF)
            rows_inv[part, :, tile:] = im_far.T.astype(BF)
            for r in range(4):
                cols_t[r, part] = cols[r, part].astype(F32).T.astype(BF)
        for copy in copies[6:10]:
            copy.wait()

    prepare()

    def place(dst, lanes, v):
        hi, lo = split(v * scale)
        dst[:, 128 * lanes : 128 * (lanes + 1)] = jnp.concatenate([hi, lo, hi], axis=0)

    def expand(v):
        lanes = lax.broadcasted_iota(jnp.int32, v.shape, 1)
        hi, lo = split(v)

        def moved(x, by):
            return x if by == 0 else pltpu.roll(x, by % 128, 1)

        out = []
        for k in range(3):
            low = moved(hi, -RANK * k)
            mid = moved(lo, RANK - RANK * k)
            top = moved(hi, 2 * RANK - RANK * k)
            out.append(jnp.where(lanes < RANK, low, jnp.where(lanes < 2 * RANK, mid, top)))
        return out

    def smooth(phase, arrive):
        chunk = half // 2
        blank = jnp.zeros((128, half), BF)

        def pack(j, c):
            rows = slice(chunk * c, chunk * (c + 1))
            if phase == 0:
                first = dot(left[j, rows, :], coef3[...])
            else:
                rows = slice(chunk * (c % 2), chunk * (c % 2 + 1))
                first = dot(left_far[j, c // 2, rows, :], far3[c // 2])
            west, mid, east = (expand(first[:, 128 * t : 128 * (t + 1)]) for t in range(3))
            pairs = [jnp.concatenate([west[k], east[k]], axis=1) for k in range(3)]
            return jnp.concatenate(mid, axis=0), jnp.concatenate(pairs, axis=0)

        def add(j, c, mid, pairs):
            rows = slice(chunk * c, chunk * (c + 1))
            table = right[j]
            both = jnp.concatenate(
                [
                    jnp.concatenate([table[:, half:], blank], axis=1),
                    jnp.concatenate([blank, table[:, :half]], axis=1),
                ],
                axis=0,
            )
            for at, got in ((0, dot(mid, table)), (tile, dot(pairs, both))):
                new = None if j == 0 else win[phase, rows, at : at + tile]
                for k in range(3):
                    cut = GAIN * jnp.abs(weights[k]) * thr_ref[j, k]
                    term = soft(got[chunk * k : chunk * (k + 1)], cut)
                    new = term if new is None else new + term
                win[phase, rows, at : at + tile] = new

        def model(j):
            at = pl.multiple_of(me * slab, slab)
            mine = expand(dot(left[j, pl.ds(at, slab), :], own3[...]))
            got = dot(jnp.concatenate(mine, axis=0), right[j])
            for k in range(3):
                term = GAIN * soft(got[slab * k : slab * (k + 1)], thr_ref[j, k])
                model_out[k] += term

        items = [(j, pair) for pair in ((0, 1), (2, 3)) for j in range(levels)]
        packed = {}
        for step in range(len(items) + 1):
            if step % levels == 0 and step < len(items):
                arrive(step // levels)
            for i in range(2):
                if step < len(items):
                    j, pair = items[step]
                    packed[step, i] = pack(j, pair[i])
                if step > 0:
                    j, pair = items[step - 1]
                    add(j, pair[i], *packed.pop((step - 1, i)))
            if phase == 0 and step < levels:
                model(step)

    def masked(cyc, phase, bands_of_rows):
        rows = []
        for at, (dr, qr) in enumerate(bands_of_rows):
            blocks = []
            for (dc, qc), src in (((-1, 1), tile), ((0, 0), 0), ((0, 1), half), ((1, 0), tile + half)):
                q = 2 * qr + qc
                if dr == 0:
                    flag = sky_buf[cyc, near_slot(dc), q : q + 1, 127:128]
                else:
                    flag = far_in[cyc, far_slot(dr, dc), q : q + 1, 127:128]
                blocks.append(win[phase, half * at : half * (at + 1), src : src + half] * flag)
            rows.append(jnp.concatenate(blocks, axis=1))
        return split(jnp.concatenate(rows, axis=0))

    def cycle(cyc, carry):
        for d in range(1, bands):
            band_copy(cyc, d).wait_recv()
        sums = []
        for k in range(3):
            total = weights[k] * gather[cyc, 0]
            for d in range(1, bands):
                total = total + weight_ref[k, (me - d + bands) % bands] * gather[cyc, d]
            sums.append(total)
        groups = []
        for g in range(3):
            out = jnp.zeros((16, 128), F32)
            for k in range(3):
                moved = sums[k]
                if k != g:
                    moved = pltpu.roll(moved, (RANK * (k - g)) % 128, 1)
                ours = (lane16 >= RANK * k) & (lane16 < RANK * (k + 1))
                out = jnp.where(ours, moved, out)
            groups.append(out)
        full = jnp.concatenate(groups, axis=0)
        o_hi, o_lo = split(full)
        stacked = jnp.concatenate([o_hi, o_lo, o_hi], axis=0)
        less = dot(reduce[...], stacked)
        for i in range(2):
            far_out[cyc, i] = with_flags(less[FAR_RANK * i : FAR_RANK * (i + 1)])
        send(cyc, FAR)
        sky_buf[cyc, 0] = with_flags(full)
        send(cyc, NEAR)
        own3[...] = stacked
        place(coef3, 1, full)
        receive(cyc, NEAR)
        for dr, dc in NEAR:
            place(coef3, dc + 1, sky_buf[cyc, near_slot(dc)])
        smooth(0, lambda i: None)
        w_hi, w_lo = masked(cyc, 0, [(0, 0), (0, 1)])
        inner = slice(half, half + tile)
        spec[...] = const_data(rows_fwd[0, :, inner], rows_fwd[1, :, inner], w_hi, w_lo)

        def arrive(i):
            group = (FAR[3:], FAR[:3])[i]
            receive(cyc, group)
            for dr, dc in group:
                place(far3.at[(dr + 1) // 2], dc + 1, far_in[cyc, far_slot(dr, dc)])

        smooth(1, arrive)
        w_hi, w_lo = masked(cyc, 1, [(-1, 1), (1, 0)])

        w_rows = jnp.concatenate([w_hi, w_lo, w_hi], axis=0)
        part_rows = half

        def freqs(c):
            return [slice(at + part_rows * c, at + part_rows * (c + 1)) for at in (0, tile)]

        def start(c):
            def outer(part):
                return jnp.concatenate(
                    [
                        jnp.concatenate(
                            [rows_fwd[part, f, :half], rows_fwd[part, f, half + tile :]], axis=1
                        )
                        for f in freqs(c)
                    ],
                    axis=0,
                )

            hi = outer(0)
            got = dot(jnp.concatenate([hi, hi, outer(1)], axis=1), w_rows)
            re, im = (
                got[part_rows * i : part_rows * (i + 1)] + spec[f, :]
                for i, f in enumerate(freqs(c))
            )
            blocks = [[v[:, half * m : half * (m + 1)] for m in range(4)] for v in (re, im)]
            return [split(v) for v in residues(*blocks)]

        def along(pair, r):
            return data_const(*pair, cols[r, 0], cols[r, 1])

        def back(r, x):
            x_re, x_im = x[:, :half], x[:, half:]
            b_re, b_im = beam_f[r, :, :half], beam_f[r, :, half:]
            hi, lo = split(
                jnp.concatenate([x_re * b_re - x_im * b_im, x_re * b_im + x_im * b_re], axis=1)
            )
            return data_const(hi, lo, cols_t[r, 0], cols_t[r, 1])

        first, second = start(0), start(1)
        x, t = [], []
        for r in range(4):
            pair = [jnp.concatenate([first[r][i], second[r][i]], axis=0) for i in range(2)]
            x.append(along(pair, r))
            if r > 0:
                t.append(back(r - 1, x[r - 1]))
        t.append(back(3, x[3]))
        even, odd, gap, turn = t[0] + t[2], t[1] + t[3], t[0] - t[2], t[1] - t[3]
        z_re = jnp.concatenate(
            [even[:, :half] - odd[:, :half], gap[:, :half] + turn[:, half:]], axis=1
        )
        z_im = jnp.concatenate(
            [even[:, half:] - odd[:, half:], gap[:, half:] - turn[:, :half]], axis=1
        )
        z_hi, z_lo = split(jnp.concatenate([z_re, z_im], axis=0))
        res_out[...] = res_out[...] - const_data(rows_inv[0], rows_inv[1], z_hi, z_lo)

        @pl.when(cyc + 1 < CYCLES)
        def _():
            compress(cyc + 1)

        return carry

    lax.fori_loop(0, CYCLES, cycle, 0)
    for cyc in range(CYCLES):
        for d in range(1, bands):
            band_copy(cyc, d).wait_send()
        for dr, dc in NEAR + FAR:

            @pl.when(inside(dr, dc))
            def _():
                sky_copy(cyc, dr, dc).wait_send()


def finish(model_in, res_in, model_out, res_out):
    model_out[...] = model_in[...]
    res_out[...] = res_in[...]


def on_device(residual_start, beam_pattern, spec_weights, thresholds, block_ids, block_counts):
    bands = lax.axis_size("band")
    sky = lax.axis_size("sky")
    tile = residual_start.shape[-1]
    coefs = spec_weights.shape[1]
    levels = thresholds.shape[0]
    tables = host_tables(tile, levels)
    vmem = pl.BlockSpec(memory_space=pltpu.VMEM)
    hbm = pl.BlockSpec(memory_space=pl.ANY)
    region = 2 * tile
    shapes = (
        jax.ShapeDtypeStruct((coefs, tile // bands, tile), F32),
        jax.ShapeDtypeStruct((tile, tile), F32),
    )
    model, res = pl.pallas_call(
        functools.partial(kernel, bands, sky),
        out_shape=shapes,
        in_specs=[hbm] * 14,
        out_specs=(vmem, vmem),
        scratch_shapes=[
            pltpu.SMEM((4,), jnp.int32),
            pltpu.SMEM((1,), jnp.int32),
            pltpu.SMEM((coefs, bands), F32),
            pltpu.SMEM((levels, coefs), F32),
            pltpu.VMEM((tile, tile), F32),
        ]
        + [pltpu.VMEM(t.shape, BF) for t in tables]
        + [
            pltpu.VMEM((2, region, region), BF),
            pltpu.VMEM((2, tile, region), BF),
            pltpu.VMEM((4, 2, tile, tile), BF),
            pltpu.VMEM((CYCLES, bands, 16, 128), F32),
            pltpu.VMEM((CYCLES, 3, KPAD, 128), F32),
            pltpu.VMEM((CYCLES, 2, FAR_RANK, 128), F32),
            pltpu.VMEM((CYCLES, 6, FAR_RANK, 128), F32),
            pltpu.VMEM((3 * KPAD, 384), BF),
            pltpu.VMEM((2, 3 * FAR_RANK, 384), BF),
            pltpu.VMEM((3 * KPAD, 128), BF),
            pltpu.VMEM((2, tile, region), F32),
            pltpu.VMEM((region, region), F32),
            pltpu.VMEM((4, tile, tile), F32),
            pltpu.SemaphoreType.DMA((14,)),
            pltpu.SemaphoreType.DMA((CYCLES, bands)),
            pltpu.SemaphoreType.DMA((CYCLES, bands)),
            pltpu.SemaphoreType.DMA((CYCLES, 9)),
            pltpu.SemaphoreType.DMA((CYCLES, 9)),
        ],
        compiler_params=pltpu.CompilerParams(
            collective_id=0, has_side_effects=True, vmem_limit_bytes=32 << 20
        ),
    )(
        pltpu.with_memory_space_constraint(block_ids[0, 0], pltpu.HBM),
        block_counts[0],
        *[
            pltpu.with_memory_space_constraint(x, pltpu.HBM)
            for x in (
                spec_weights.T,
                thresholds,
                residual_start[0, 0],
                beam_pattern[0],
                *[jnp.asarray(t) for t in tables],
            )
        ],
    )
    model, res = pl.pallas_call(
        finish,
        out_shape=shapes,
        in_specs=[vmem] * 2,
        out_specs=(vmem, vmem),
        compiler_params=pltpu.CompilerParams(vmem_limit_bytes=4 << 20),
    )(model, res)
    return (model[:, None], res[None, None])


def solution(mesh):
    placed = (
        P("band", "sky", None, None),
        P("band", None, None),
        P(),
        P(),
        P("band", "sky", None),
        P("band", "sky"),
    )
    return jax.shard_map(
        on_device,
        mesh=mesh,
        in_specs=placed,
        out_specs=(P(None, "sky", "band", None), P("band", "sky", None, None)),
        check_vma=False,
    )
```

```python
import functools

import jax
import jax.numpy as jnp
import numpy as np
from jax import lax
from jax.experimental import pallas as pl
from jax.experimental.pallas import tpu as pltpu
from jax.sharding import PartitionSpec as P

CYCLES = 2
TGX = 4
GAIN = 0.25
RANK = 42
KPAD = 48
AHEAD = 4
FAR_RANK = 32
MESH = pl.DeviceIdType.MESH
BF = jnp.bfloat16
F32 = jnp.float32


def host_split(a):
    hi = np.asarray(a, np.float64).astype(BF)
    lo = (np.asarray(a, np.float64) - hi.astype(np.float64)).astype(BF)
    return hi, lo


def host_tables(tile, levels):
    pos = np.arange(tile, dtype=np.float64)
    off = pos[:, None] - pos[None, :]
    smooth = []
    for j in range(levels):
        spread = 2.0**j * tile / 16.0
        k = np.exp(-off * off / (2.0 * spread * spread))
        smooth.append(k / np.sqrt(np.sum(k * k, axis=1, keepdims=True)))
    smooth = np.stack(smooth)
    _, _, vt = np.linalg.svd(smooth.reshape(-1, tile), full_matrices=False)
    basis = vt[:RANK].T
    proj = np.zeros((tile, 128))
    proj[:, :RANK] = basis
    proj_t = np.zeros((KPAD, tile))
    proj_t[:RANK] = basis.T
    expand = smooth @ basis

    p_hi, p_lo = host_split(proj)
    t_hi, t_lo = host_split(proj_t)
    project = np.concatenate([p_hi, p_hi, p_lo], axis=0)
    project_t = np.concatenate([t_hi, t_hi, t_lo], axis=1)

    left = np.zeros((levels, tile, KPAD))
    left[:, :, :RANK] = expand
    l_hi, l_lo = host_split(left)
    left3 = np.concatenate([l_hi, l_hi, l_lo], axis=2)

    far, reduce = [], np.zeros((2 * FAR_RANK, KPAD))
    for i, rows in enumerate((slice(tile // 2, tile), slice(0, tile // 2))):
        _, _, vt = np.linalg.svd(expand[:, rows].reshape(-1, RANK), full_matrices=False)
        reduce[FAR_RANK * i : FAR_RANK * (i + 1), :RANK] = vt[:FAR_RANK]
        f_hi, f_lo = host_split(expand[:, rows] @ vt[:FAR_RANK].T)
        far.append(np.concatenate([f_hi, f_hi, f_lo], axis=2))
    left_far = np.stack(far, axis=1)
    z_hi, z_lo = host_split(reduce)
    reduce3 = np.concatenate([z_hi, z_hi, z_lo], axis=1)

    right = np.zeros((levels, 128, tile), BF)
    g_hi, g_lo = host_split(expand.transpose(0, 2, 1))
    for p, g in enumerate((g_hi, g_hi, g_lo)):
        right[:, RANK * p : RANK * (p + 1)] = g

    n = 2 * tile
    f = np.arange(tile) + 0.5
    ang = 2.0 * np.pi * f[:, None] * np.arange(tile)[None, :] / n
    rows_fwd = np.stack(host_split(np.concatenate([np.cos(ang), -np.sin(ang)], axis=0)))

    cols = []
    x = np.arange(tile // 2)
    for r in range(4):
        a = 2.0 * np.pi * x[:, None] * (4 * x[None, :] + r) / n
        c, s = np.cos(a), np.sin(a)
        cols.append(np.stack(host_split(np.block([[c, -s], [s, c]]))))
    cols = np.stack(cols)
    return project_t, project, reduce3, rows_fwd, cols, left3, right, left_far


def split(v):
    hi = v.astype(BF)
    return hi, (v - hi.astype(F32)).astype(BF)


def dot(a, b):
    return jnp.dot(a, b, preferred_element_type=F32)


def data_const(hi, lo, c_hi, c_lo):
    return dot(jnp.concatenate([hi, lo, hi], axis=1), jnp.concatenate([c_hi, c_hi, c_lo], axis=0))


def const_data(c_hi, c_lo, hi, lo):
    return dot(jnp.concatenate([c_hi, c_hi, c_lo], axis=1), jnp.concatenate([hi, lo, hi], axis=0))


def soft(v, t):
    return v - jnp.minimum(jnp.maximum(v, -t), t)


def residues(re, im):
    (a_re, b_re, c_re, d_re), (a_im, b_im, c_im, d_im) = (
        (v[0] + v[2], v[1] + v[3], v[0] - v[2], v[1] - v[3]) for v in (re, im)
    )
    return [
        jnp.concatenate(pair, axis=1)
        for pair in (
            (a_re + b_re, a_im + b_im),
            (c_re + d_im, c_im - d_re),
            (a_re - b_re, a_im - b_im),
            (c_re - d_im, c_im + d_re),
        )
    ]


NEAR = [(0, 1), (0, -1)]
FAR = [(1, 1), (1, -1), (1, 0), (-1, 0), (-1, 1), (-1, -1)]


def kernel(
    bands,
    sky,
    ids_hbm,
    count_hbm,
    weight_hbm,
    thr_hbm,
    res_hbm,
    beam_hbm,
    project_t_hbm,
    project_hbm,
    reduce_hbm,
    rows_hbm,
    cols_hbm,
    left_hbm,
    right_hbm,
    left_far_hbm,
    model_out,
    res_out,
    ids_ref,
    count_ref,
    weight_ref,
    thr_ref,
    beam,
    project_t,
    project,
    reduce,
    rows_half,
    cols,
    left,
    right,
    left_far,
    rows_fwd,
    rows_inv,
    cols_t,
    gather,
    sky_buf,
    far_out,
    far_in,
    coef3,
    far3,
    own3,
    win,
    spec,
    beam_f,
    const_sem,
    band_send,
    band_recv,
    sky_send,
    sky_recv,
):
    tile = res_out.shape[0]
    half = tile // 2
    levels = left.shape[0]
    slab = tile // bands
    sky_rows = sky // TGX
    me = lax.axis_index("band")
    spot = lax.axis_index("sky")
    row, col = spot // TGX, spot % TGX

    def sky_id(dr, dc):
        return ((row + dr + sky_rows) % sky_rows) * TGX + (col + dc + TGX) % TGX

    pairs = [
        (res_hbm, res_out),
        (project_t_hbm, project_t),
        (project_hbm, project),
        (beam_hbm, beam),
        (rows_hbm, rows_half),
        (cols_hbm, cols),
        (reduce_hbm, reduce),
        (left_hbm, left),
        (right_hbm, right),
        (left_far_hbm, left_far),
        (ids_hbm, ids_ref),
        (count_hbm, count_ref),
        (weight_hbm, weight_ref),
        (thr_hbm, thr_ref),
    ]
    copies = [
        pltpu.make_async_copy(src, dst, const_sem.at[i]) for i, (src, dst) in enumerate(pairs)
    ]
    for copy in copies[:3]:
        copy.start()

    barrier = pltpu.get_barrier_semaphore()
    for d in range(1, bands):
        pl.semaphore_signal(
            barrier, inc=1, device_id={"band": (me + d) % bands}, device_id_type=MESH
        )
    for dr, dc in NEAR + FAR:
        pl.semaphore_signal(barrier, inc=1, device_id={"sky": sky_id(dr, dc)}, device_id_type=MESH)

    for copy in copies[3:]:
        copy.start()

    def band_copy(cyc, d):
        return pltpu.make_async_remote_copy(
            src_ref=gather.at[cyc, 0],
            dst_ref=gather.at[cyc, d],
            send_sem=band_send.at[cyc, d],
            recv_sem=band_recv.at[cyc, d],
            device_id={"band": (me + d) % bands},
            device_id_type=MESH,
        )

    def compress(cyc):
        r_hi, r_lo = split(res_out[...])
        part = dot(project_t[...], jnp.concatenate([r_hi, r_lo, r_hi], axis=0))
        p_hi, p_lo = split(part)
        coef = dot(jnp.concatenate([p_hi, p_lo, p_hi], axis=1), project[...])
        gather[cyc, 0] = (
            coef[0:16] + pltpu.roll(coef[16:32], RANK, 1) + pltpu.roll(coef[32:48], 2 * RANK, 1)
        )
        if isinstance(cyc, int):
            pl.semaphore_wait(barrier, bands - 1 + 8)
        for d in sorted(range(1, bands), key=lambda d: (-min(d // 2, (bands - d) // 2), d % 2)):
            band_copy(cyc, d).start()

    for copy in copies[:3]:
        copy.wait()
    compress(0)

    model_out[...] = jnp.zeros_like(model_out)

    lane = lax.broadcasted_iota(jnp.int32, (1, 128), 1)
    lane16 = lax.broadcasted_iota(jnp.int32, (16, 128), 1)
    for copy in copies[10:]:
        copy.wait()
    flags = []
    for q in range(4):
        live = jnp.float32(0.0)
        for s in range(4):
            hit = jnp.where(ids_ref[s] == q, 1.0, 0.0) * jnp.where(s < count_ref[0], 1.0, 0.0)
            live = live + hit
        flags.append(live)
    weights = [weight_ref[k, me] for k in range(3)]
    scale = jnp.zeros((1, 128), F32)
    for k in range(3):
        ours = (lane >= RANK * k) & (lane < RANK * (k + 1))
        scale = jnp.where(ours, GAIN * weights[k], scale)

    def near_slot(dc):
        return (dc + 3) % 3

    def sky_copy(cyc, dr, dc):
        if dr == 0:
            src, dst = sky_buf.at[cyc, 0], sky_buf.at[cyc, near_slot(-dc)]
        else:
            src, dst = far_out.at[cyc, (1 - dr) // 2], far_in.at[cyc, far_slot(-dr, -dc)]
        slot = (1 - dr) * 3 + (1 - dc)
        return pltpu.make_async_remote_copy(
            src_ref=src,
            dst_ref=dst,
            send_sem=sky_send.at[cyc, slot],
            recv_sem=sky_recv.at[cyc, slot],
            device_id={"sky": sky_id(dr, dc)},
            device_id_type=MESH,
        )

    def far_slot(dr, dc):
        return (dr + 1) // 2 * 3 + dc + 1

    def inside(dr, dc):
        return (row + dr >= 0) & (row + dr < sky_rows) & (col + dc >= 0) & (col + dc < TGX)

    for dr, dc in NEAR + FAR:

        @pl.when(jnp.logical_not(inside(dr, dc)))
        def _():
            for cyc in range(CYCLES):
                if dr == 0:
                    sky_buf[cyc, near_slot(dc)] = jnp.zeros((KPAD, 128), F32)
                else:
                    far_in[cyc, far_slot(dr, dc)] = jnp.zeros((FAR_RANK, 128), F32)

    def send(cyc, where):
        for dr, dc in where:

            @pl.when(inside(dr, dc))
            def _():
                sky_copy(cyc, dr, dc).start()

    def receive(cyc, where):
        for dr, dc in where:

            @pl.when(inside(dr, dc))
            def _():
                sky_copy(cyc, -dr, -dc).wait_recv()

    def with_flags(v):
        r = lax.broadcasted_iota(jnp.int32, v.shape, 0)
        c = lax.broadcasted_iota(jnp.int32, v.shape, 1)
        for q in range(4):
            v = jnp.where((c == 127) & (r == q), flags[q], v)
        return v

    def prepare():
        for copy in copies[3:6]:
            copy.wait()
        alt = (1 - 2 * (lax.broadcasted_iota(jnp.int32, (tile, 1), 0) % 2)).astype(F32)
        b_hi, b_lo = split(beam[...])
        first = const_data(rows_half[0], rows_half[1], b_hi, b_lo)
        blank = jnp.zeros((tile, half), F32)
        re, im = (
            [first[at : at + tile, :half], first[at : at + tile, half:], blank, blank]
            for at in (0, tile)
        )
        norm = 2.0 / (4 * tile * tile)
        for r, v in enumerate(residues(re, im)):
            hi, lo = split(v)
            beam_f[r] = norm * data_const(hi, lo, cols[r, 0], cols[r, 1])
        for part in range(2):
            re = rows_half[part, :tile].astype(F32)
            im = rows_half[part, tile:].astype(F32)
            re_far, im_far = im * alt, -(re * alt)
            rows_fwd[part, :, :tile] = rows_half[part]
            rows_fwd[part, :tile, tile:] = re_far.astype(BF)
            rows_fwd[part, tile:, tile:] = im_far.astype(BF)
            rows_inv[part, :, :tile] = re_far.T.astype(BF)
            rows_inv[part, :, tile:] = im_far.T.astype(BF)
            for r in range(4):
                cols_t[r, part] = cols[r, part].astype(F32).T.astype(BF)
        for copy in copies[6:10]:
            copy.wait()

    prepare()

    def place(dst, lanes, v):
        hi, lo = split(v * scale)
        dst[:, 128 * lanes : 128 * (lanes + 1)] = jnp.concatenate([hi, lo, hi], axis=0)

    def expand(v):
        lanes = lax.broadcasted_iota(jnp.int32, v.shape, 1)
        hi, lo = split(v)

        def moved(x, by):
            return x if by == 0 else pltpu.roll(x, by % 128, 1)

        out = []
        for k in range(3):
            low = moved(hi, -RANK * k)
            mid = moved(lo, RANK - RANK * k)
            top = moved(hi, 2 * RANK - RANK * k)
            out.append(jnp.where(lanes < RANK, low, jnp.where(lanes < 2 * RANK, mid, top)))
        return out

    def smooth(phase):
        chunk = half // 2
        blank = jnp.zeros((128, half), BF)

        def pack(j, c):
            rows = slice(chunk * c, chunk * (c + 1))
            if phase == 0:
                first = dot(left[j, rows, :], coef3[...])
            else:
                rows = slice(chunk * (c % 2), chunk * (c % 2 + 1))
                first = dot(left_far[j, c // 2, rows, :], far3[c // 2])
            west, mid, east = (expand(first[:, 128 * t : 128 * (t + 1)]) for t in range(3))
            pairs = [jnp.concatenate([west[k], east[k]], axis=1) for k in range(3)]
            return jnp.concatenate(mid, axis=0), jnp.concatenate(pairs, axis=0)

        def add(j, c, mid, pairs):
            rows = slice(chunk * c, chunk * (c + 1))
            table = right[j]
            both = jnp.concatenate(
                [
                    jnp.concatenate([table[:, half:], blank], axis=1),
                    jnp.concatenate([blank, table[:, :half]], axis=1),
                ],
                axis=0,
            )
            for at, got in ((0, dot(mid, table)), (tile, dot(pairs, both))):
                new = None if j == 0 else win[phase, rows, at : at + tile]
                for k in range(3):
                    cut = GAIN * jnp.abs(weights[k]) * thr_ref[j, k]
                    term = soft(got[chunk * k : chunk * (k + 1)], cut)
                    new = term if new is None else new + term
                win[phase, rows, at : at + tile] = new

        def model(j):
            at = pl.multiple_of(me * slab, slab)
            mine = expand(dot(left[j, pl.ds(at, slab), :], own3[...]))
            got = dot(jnp.concatenate(mine, axis=0), right[j])
            for k in range(3):
                term = GAIN * soft(got[slab * k : slab * (k + 1)], thr_ref[j, k])
                model_out[k] += term

        items = [(j, c) for j in range(levels) for c in range(4)]
        packed = {}
        for step in range(0, len(items) + AHEAD, AHEAD):
            for i in range(step, step + AHEAD):
                if i >= AHEAD:
                    add(*items[i - AHEAD], *packed.pop(i - AHEAD))
                if i < len(items):
                    packed[i] = pack(*items[i])
            if phase == 0 and step < AHEAD * levels and step % AHEAD == 0:
                model(step // AHEAD)

    def masked(cyc, phase, bands_of_rows):
        rows = []
        for at, (dr, qr) in enumerate(bands_of_rows):
            blocks = []
            for (dc, qc), src in (((-1, 1), tile), ((0, 0), 0), ((0, 1), half), ((1, 0), tile + half)):
                q = 2 * qr + qc
                if dr == 0:
                    flag = sky_buf[cyc, near_slot(dc), q : q + 1, 127:128]
                else:
                    flag = far_in[cyc, far_slot(dr, dc), q : q + 1, 127:128]
                blocks.append(win[phase, half * at : half * (at + 1), src : src + half] * flag)
            rows.append(jnp.concatenate(blocks, axis=1))
        return split(jnp.concatenate(rows, axis=0))

    def cycle(cyc, carry):
        for d in range(1, bands):
            band_copy(cyc, d).wait_recv()
        sums = []
        for k in range(3):
            total = weights[k] * gather[cyc, 0]
            for d in range(1, bands):
                total = total + weight_ref[k, (me - d + bands) % bands] * gather[cyc, d]
            sums.append(total)
        groups = []
        for g in range(3):
            out = jnp.zeros((16, 128), F32)
            for k in range(3):
                moved = sums[k]
                if k != g:
                    moved = pltpu.roll(moved, (RANK * (k - g)) % 128, 1)
                ours = (lane16 >= RANK * k) & (lane16 < RANK * (k + 1))
                out = jnp.where(ours, moved, out)
            groups.append(out)
        full = jnp.concatenate(groups, axis=0)
        o_hi, o_lo = split(full)
        stacked = jnp.concatenate([o_hi, o_lo, o_hi], axis=0)
        less = dot(reduce[...], stacked)
        for i in range(2):
            far_out[cyc, i] = with_flags(less[FAR_RANK * i : FAR_RANK * (i + 1)])
        send(cyc, FAR)
        sky_buf[cyc, 0] = with_flags(full)
        send(cyc, NEAR)
        own3[...] = stacked
        place(coef3, 1, full)
        receive(cyc, NEAR)
        for dr, dc in NEAR:
            place(coef3, dc + 1, sky_buf[cyc, near_slot(dc)])
        smooth(0)
        w_hi, w_lo = masked(cyc, 0, [(0, 0), (0, 1)])
        inner = slice(half, half + tile)
        spec[...] = const_data(rows_fwd[0, :, inner], rows_fwd[1, :, inner], w_hi, w_lo)

        receive(cyc, FAR)
        for dr, dc in FAR:
            place(far3.at[(dr + 1) // 2], dc + 1, far_in[cyc, far_slot(dr, dc)])
        smooth(1)
        w_hi, w_lo = masked(cyc, 1, [(-1, 1), (1, 0)])

        w_rows = jnp.concatenate([w_hi, w_lo, w_hi], axis=0)
        part_rows = half

        def freqs(c):
            return [slice(at + part_rows * c, at + part_rows * (c + 1)) for at in (0, tile)]

        def start(c):
            def outer(part):
                return jnp.concatenate(
                    [
                        jnp.concatenate(
                            [rows_fwd[part, f, :half], rows_fwd[part, f, half + tile :]], axis=1
                        )
                        for f in freqs(c)
                    ],
                    axis=0,
                )

            hi = outer(0)
            got = dot(jnp.concatenate([hi, hi, outer(1)], axis=1), w_rows)
            re, im = (
                got[part_rows * i : part_rows * (i + 1)] + spec[f, :]
                for i, f in enumerate(freqs(c))
            )
            blocks = [[v[:, half * m : half * (m + 1)] for m in range(4)] for v in (re, im)]
            return [split(v) for v in residues(*blocks)]

        def along(pair, r):
            return data_const(*pair, cols[r, 0], cols[r, 1])

        def back(r, x):
            x_re, x_im = x[:, :half], x[:, half:]
            b_re, b_im = beam_f[r, :, :half], beam_f[r, :, half:]
            hi, lo = split(
                jnp.concatenate([x_re * b_re - x_im * b_im, x_re * b_im + x_im * b_re], axis=1)
            )
            return data_const(hi, lo, cols_t[r, 0], cols_t[r, 1])

        first, second = start(0), start(1)
        x, t = [], []
        for r in range(4):
            pair = [jnp.concatenate([first[r][i], second[r][i]], axis=0) for i in range(2)]
            x.append(along(pair, r))
            if r > 0:
                t.append(back(r - 1, x[r - 1]))
        t.append(back(3, x[3]))
        even, odd, gap, turn = t[0] + t[2], t[1] + t[3], t[0] - t[2], t[1] - t[3]
        z_re = jnp.concatenate(
            [even[:, :half] - odd[:, :half], gap[:, :half] + turn[:, half:]], axis=1
        )
        z_im = jnp.concatenate(
            [even[:, half:] - odd[:, half:], gap[:, half:] - turn[:, :half]], axis=1
        )
        z_hi, z_lo = split(jnp.concatenate([z_re, z_im], axis=0))
        res_out[...] = res_out[...] - const_data(rows_inv[0], rows_inv[1], z_hi, z_lo)

        @pl.when(cyc + 1 < CYCLES)
        def _():
            compress(cyc + 1)

        return carry

    lax.fori_loop(0, CYCLES, cycle, 0)
    for cyc in range(CYCLES):
        for d in range(1, bands):
            band_copy(cyc, d).wait_send()
        for dr, dc in NEAR + FAR:

            @pl.when(inside(dr, dc))
            def _():
                sky_copy(cyc, dr, dc).wait_send()


def finish(model_in, res_in, model_out, res_out):
    model_out[...] = model_in[...]
    res_out[...] = res_in[...]


def on_device(residual_start, beam_pattern, spec_weights, thresholds, block_ids, block_counts):
    bands = lax.axis_size("band")
    sky = lax.axis_size("sky")
    tile = residual_start.shape[-1]
    coefs = spec_weights.shape[1]
    levels = thresholds.shape[0]
    tables = host_tables(tile, levels)
    vmem = pl.BlockSpec(memory_space=pltpu.VMEM)
    hbm = pl.BlockSpec(memory_space=pl.ANY)
    region = 2 * tile
    shapes = (
        jax.ShapeDtypeStruct((coefs, tile // bands, tile), F32),
        jax.ShapeDtypeStruct((tile, tile), F32),
    )
    model, res = pl.pallas_call(
        functools.partial(kernel, bands, sky),
        out_shape=shapes,
        in_specs=[hbm] * 14,
        out_specs=(vmem, vmem),
        scratch_shapes=[
            pltpu.SMEM((4,), jnp.int32),
            pltpu.SMEM((1,), jnp.int32),
            pltpu.SMEM((coefs, bands), F32),
            pltpu.SMEM((levels, coefs), F32),
            pltpu.VMEM((tile, tile), F32),
        ]
        + [pltpu.VMEM(t.shape, BF) for t in tables]
        + [
            pltpu.VMEM((2, region, region), BF),
            pltpu.VMEM((2, tile, region), BF),
            pltpu.VMEM((4, 2, tile, tile), BF),
            pltpu.VMEM((CYCLES, bands, 16, 128), F32),
            pltpu.VMEM((CYCLES, 3, KPAD, 128), F32),
            pltpu.VMEM((CYCLES, 2, FAR_RANK, 128), F32),
            pltpu.VMEM((CYCLES, 6, FAR_RANK, 128), F32),
            pltpu.VMEM((3 * KPAD, 384), BF),
            pltpu.VMEM((2, 3 * FAR_RANK, 384), BF),
            pltpu.VMEM((3 * KPAD, 128), BF),
            pltpu.VMEM((2, tile, region), F32),
            pltpu.VMEM((region, region), F32),
            pltpu.VMEM((4, tile, tile), F32),
            pltpu.SemaphoreType.DMA((14,)),
            pltpu.SemaphoreType.DMA((CYCLES, bands)),
            pltpu.SemaphoreType.DMA((CYCLES, bands)),
            pltpu.SemaphoreType.DMA((CYCLES, 9)),
            pltpu.SemaphoreType.DMA((CYCLES, 9)),
        ],
        compiler_params=pltpu.CompilerParams(
            collective_id=0, has_side_effects=True, vmem_limit_bytes=32 << 20
        ),
    )(
        pltpu.with_memory_space_constraint(block_ids[0, 0], pltpu.HBM),
        block_counts[0],
        *[
            pltpu.with_memory_space_constraint(x, pltpu.HBM)
            for x in (
                spec_weights.T,
                thresholds,
                residual_start[0, 0],
                beam_pattern[0],
                *[jnp.asarray(t) for t in tables],
            )
        ],
    )
    model, res = pl.pallas_call(
        finish,
        out_shape=shapes,
        in_specs=[vmem] * 2,
        out_specs=(vmem, vmem),
        compiler_params=pltpu.CompilerParams(vmem_limit_bytes=4 << 20),
    )(model, res)
    return (model[:, None], res[None, None])


def solution(mesh):
    placed = (
        P("band", "sky", None, None),
        P("band", None, None),
        P(),
        P(),
        P("band", "sky", None),
        P("band", "sky"),
    )
    return jax.shard_map(
        on_device,
        mesh=mesh,
        in_specs=placed,
        out_specs=(P(None, "sky", "band", None), P("band", "sky", None, None)),
        check_vma=False,
    )
```

```python
import functools

import jax
import jax.numpy as jnp
import numpy as np
from jax import lax
from jax.experimental import pallas as pl
from jax.experimental.pallas import tpu as pltpu
from jax.sharding import PartitionSpec as P

CYCLES = 2
TGX = 4
GAIN = 0.25
RANK = 42
KPAD = 48
AHEAD = 4
FAR_RANK = 32
MESH = pl.DeviceIdType.MESH
BF = jnp.bfloat16
F32 = jnp.float32


def host_split(a):
    hi = np.asarray(a, np.float64).astype(BF)
    lo = (np.asarray(a, np.float64) - hi.astype(np.float64)).astype(BF)
    return hi, lo


def host_tables(tile, levels):
    pos = np.arange(tile, dtype=np.float64)
    off = pos[:, None] - pos[None, :]
    smooth = []
    for j in range(levels):
        spread = 2.0**j * tile / 16.0
        k = np.exp(-off * off / (2.0 * spread * spread))
        smooth.append(k / np.sqrt(np.sum(k * k, axis=1, keepdims=True)))
    smooth = np.stack(smooth)
    _, _, vt = np.linalg.svd(smooth.reshape(-1, tile), full_matrices=False)
    basis = vt[:RANK].T
    proj = np.zeros((tile, 128))
    proj[:, :RANK] = basis
    proj_t = np.zeros((KPAD, tile))
    proj_t[:RANK] = basis.T
    expand = smooth @ basis

    p_hi, p_lo = host_split(proj)
    t_hi, t_lo = host_split(proj_t)
    project = np.concatenate([p_hi, p_hi, p_lo], axis=0)
    project_t = np.concatenate([t_hi, t_hi, t_lo], axis=1)

    left = np.zeros((levels, tile, KPAD))
    left[:, :, :RANK] = expand
    l_hi, l_lo = host_split(left)
    left3 = np.concatenate([l_hi, l_hi, l_lo], axis=2)

    far, reduce = [], np.zeros((2 * FAR_RANK, KPAD))
    for i, rows in enumerate((slice(tile // 2, tile), slice(0, tile // 2))):
        _, _, vt = np.linalg.svd(expand[:, rows].reshape(-1, RANK), full_matrices=False)
        reduce[FAR_RANK * i : FAR_RANK * (i + 1), :RANK] = vt[:FAR_RANK]
        f_hi, f_lo = host_split(expand[:, rows] @ vt[:FAR_RANK].T)
        far.append(np.concatenate([f_hi, f_hi, f_lo], axis=2))
    left_far = np.stack(far, axis=1)
    z_hi, z_lo = host_split(reduce)
    reduce3 = np.concatenate([z_hi, z_hi, z_lo], axis=1)

    right = np.zeros((levels, 128, tile), BF)
    g_hi, g_lo = host_split(expand.transpose(0, 2, 1))
    for p, g in enumerate((g_hi, g_hi, g_lo)):
        right[:, RANK * p : RANK * (p + 1)] = g

    n = 2 * tile
    f = np.arange(tile) + 0.5
    ang = 2.0 * np.pi * f[:, None] * np.arange(tile)[None, :] / n
    rows_fwd = np.stack(host_split(np.concatenate([np.cos(ang), -np.sin(ang)], axis=0)))

    cols = []
    x = np.arange(tile // 2)
    for r in range(4):
        a = 2.0 * np.pi * x[:, None] * (4 * x[None, :] + r) / n
        c, s = np.cos(a), np.sin(a)
        cols.append(np.stack(host_split(np.block([[c, -s], [s, c]]))))
    cols = np.stack(cols)
    return project_t, project, reduce3, rows_fwd, cols, left3, right, left_far


def split(v):
    hi = v.astype(BF)
    return hi, (v - hi.astype(F32)).astype(BF)


def dot(a, b):
    return jnp.dot(a, b, preferred_element_type=F32)


def data_const(hi, lo, c_hi, c_lo):
    return dot(jnp.concatenate([hi, lo, hi], axis=1), jnp.concatenate([c_hi, c_hi, c_lo], axis=0))


def const_data(c_hi, c_lo, hi, lo):
    return dot(jnp.concatenate([c_hi, c_hi, c_lo], axis=1), jnp.concatenate([hi, lo, hi], axis=0))


def soft(v, t):
    return v - jnp.minimum(jnp.maximum(v, -t), t)


def residues(re, im):
    (a_re, b_re, c_re, d_re), (a_im, b_im, c_im, d_im) = (
        (v[0] + v[2], v[1] + v[3], v[0] - v[2], v[1] - v[3]) for v in (re, im)
    )
    return [
        jnp.concatenate(pair, axis=1)
        for pair in (
            (a_re + b_re, a_im + b_im),
            (c_re + d_im, c_im - d_re),
            (a_re - b_re, a_im - b_im),
            (c_re - d_im, c_im + d_re),
        )
    ]


NEAR = [(0, 1), (0, -1)]
FAR = [(1, 0), (-1, 0), (1, 1), (1, -1), (-1, 1), (-1, -1)]


def kernel(
    bands,
    sky,
    ids_hbm,
    count_hbm,
    weight_hbm,
    thr_hbm,
    res_hbm,
    beam_hbm,
    project_t_hbm,
    project_hbm,
    reduce_hbm,
    rows_hbm,
    cols_hbm,
    left_hbm,
    right_hbm,
    left_far_hbm,
    model_out,
    res_out,
    ids_ref,
    count_ref,
    weight_ref,
    thr_ref,
    beam,
    project_t,
    project,
    reduce,
    rows_half,
    cols,
    left,
    right,
    left_far,
    rows_fwd,
    rows_inv,
    cols_t,
    gather,
    sky_buf,
    far_out,
    far_in,
    coef3,
    far3,
    own3,
    win,
    spec,
    beam_f,
    const_sem,
    band_send,
    band_recv,
    sky_send,
    sky_recv,
):
    tile = res_out.shape[0]
    half = tile // 2
    levels = left.shape[0]
    slab = tile // bands
    sky_rows = sky // TGX
    me = lax.axis_index("band")
    spot = lax.axis_index("sky")
    row, col = spot // TGX, spot % TGX

    def sky_id(dr, dc):
        return ((row + dr + sky_rows) % sky_rows) * TGX + (col + dc + TGX) % TGX

    pairs = [
        (res_hbm, res_out),
        (project_t_hbm, project_t),
        (project_hbm, project),
        (beam_hbm, beam),
        (rows_hbm, rows_half),
        (cols_hbm, cols),
        (reduce_hbm, reduce),
        (left_hbm, left),
        (right_hbm, right),
        (left_far_hbm, left_far),
        (ids_hbm, ids_ref),
        (count_hbm, count_ref),
        (weight_hbm, weight_ref),
        (thr_hbm, thr_ref),
    ]
    copies = [
        pltpu.make_async_copy(src, dst, const_sem.at[i]) for i, (src, dst) in enumerate(pairs)
    ]
    for copy in copies[:3]:
        copy.start()

    barrier = pltpu.get_barrier_semaphore()
    for d in range(1, bands):
        pl.semaphore_signal(
            barrier, inc=1, device_id={"band": (me + d) % bands}, device_id_type=MESH
        )
    for dr, dc in NEAR + FAR:
        pl.semaphore_signal(barrier, inc=1, device_id={"sky": sky_id(dr, dc)}, device_id_type=MESH)

    for copy in copies[3:]:
        copy.start()

    def band_copy(cyc, d):
        return pltpu.make_async_remote_copy(
            src_ref=gather.at[cyc, 0],
            dst_ref=gather.at[cyc, d],
            send_sem=band_send.at[cyc, d],
            recv_sem=band_recv.at[cyc, d],
            device_id={"band": (me + d) % bands},
            device_id_type=MESH,
        )

    def compress(cyc):
        r_hi, r_lo = split(res_out[...])
        part = dot(project_t[...], jnp.concatenate([r_hi, r_lo, r_hi], axis=0))
        p_hi, p_lo = split(part)
        coef = dot(jnp.concatenate([p_hi, p_lo, p_hi], axis=1), project[...])
        gather[cyc, 0] = (
            coef[0:16] + pltpu.roll(coef[16:32], RANK, 1) + pltpu.roll(coef[32:48], 2 * RANK, 1)
        )
        if isinstance(cyc, int):
            pl.semaphore_wait(barrier, bands - 1 + 8)
        for d in range(1, bands):
            band_copy(cyc, d).start()

    for copy in copies[:3]:
        copy.wait()
    compress(0)

    model_out[...] = jnp.zeros_like(model_out)

    lane = lax.broadcasted_iota(jnp.int32, (1, 128), 1)
    lane16 = lax.broadcasted_iota(jnp.int32, (16, 128), 1)
    for copy in copies[10:]:
        copy.wait()
    flags = []
    for q in range(4):
        live = jnp.float32(0.0)
        for s in range(4):
            hit = jnp.where(ids_ref[s] == q, 1.0, 0.0) * jnp.where(s < count_ref[0], 1.0, 0.0)
            live = live + hit
        flags.append(live)
    weights = [weight_ref[k, me] for k in range(3)]
    scale = jnp.zeros((1, 128), F32)
    for k in range(3):
        ours = (lane >= RANK * k) & (lane < RANK * (k + 1))
        scale = jnp.where(ours, GAIN * weights[k], scale)

    def near_slot(dc):
        return (dc + 3) % 3

    def sky_copy(cyc, dr, dc):
        if dr == 0:
            src, dst = sky_buf.at[cyc, 0], sky_buf.at[cyc, near_slot(-dc)]
        else:
            src, dst = far_out.at[cyc, (1 - dr) // 2], far_in.at[cyc, far_slot(-dr, -dc)]
        slot = (1 - dr) * 3 + (1 - dc)
        return pltpu.make_async_remote_copy(
            src_ref=src,
            dst_ref=dst,
            send_sem=sky_send.at[cyc, slot],
            recv_sem=sky_recv.at[cyc, slot],
            device_id={"sky": sky_id(dr, dc)},
            device_id_type=MESH,
        )

    def far_slot(dr, dc):
        return (dr + 1) // 2 * 3 + dc + 1

    def inside(dr, dc):
        return (row + dr >= 0) & (row + dr < sky_rows) & (col + dc >= 0) & (col + dc < TGX)

    for dr, dc in NEAR + FAR:

        @pl.when(jnp.logical_not(inside(dr, dc)))
        def _():
            for cyc in range(CYCLES):
                if dr == 0:
                    sky_buf[cyc, near_slot(dc)] = jnp.zeros((KPAD, 128), F32)
                else:
                    far_in[cyc, far_slot(dr, dc)] = jnp.zeros((FAR_RANK, 128), F32)

    def send(cyc, where):
        for dr, dc in where:

            @pl.when(inside(dr, dc))
            def _():
                sky_copy(cyc, dr, dc).start()

    def receive(cyc, where):
        for dr, dc in where:

            @pl.when(inside(dr, dc))
            def _():
                sky_copy(cyc, -dr, -dc).wait_recv()

    def with_flags(v):
        r = lax.broadcasted_iota(jnp.int32, v.shape, 0)
        c = lax.broadcasted_iota(jnp.int32, v.shape, 1)
        for q in range(4):
            v = jnp.where((c == 127) & (r == q), flags[q], v)
        return v

    def prepare():
        for copy in copies[3:6]:
            copy.wait()
        alt = (1 - 2 * (lax.broadcasted_iota(jnp.int32, (tile, 1), 0) % 2)).astype(F32)
        b_hi, b_lo = split(beam[...])
        first = const_data(rows_half[0], rows_half[1], b_hi, b_lo)
        blank = jnp.zeros((tile, half), F32)
        re, im = (
            [first[at : at + tile, :half], first[at : at + tile, half:], blank, blank]
            for at in (0, tile)
        )
        norm = 2.0 / (4 * tile * tile)
        for r, v in enumerate(residues(re, im)):
            hi, lo = split(v)
            beam_f[r] = norm * data_const(hi, lo, cols[r, 0], cols[r, 1])
        for part in range(2):
            re = rows_half[part, :tile].astype(F32)
            im = rows_half[part, tile:].astype(F32)
            re_far, im_far = im * alt, -(re * alt)
            rows_fwd[part, :, :tile] = rows_half[part]
            rows_fwd[part, :tile, tile:] = re_far.astype(BF)
            rows_fwd[part, tile:, tile:] = im_far.astype(BF)
            rows_inv[part, :, :tile] = re_far.T.astype(BF)
            rows_inv[part, :, tile:] = im_far.T.astype(BF)
            for r in range(4):
                cols_t[r, part] = cols[r, part].astype(F32).T.astype(BF)
        for copy in copies[6:10]:
            copy.wait()

    prepare()

    def place(dst, lanes, v):
        hi, lo = split(v * scale)
        dst[:, 128 * lanes : 128 * (lanes + 1)] = jnp.concatenate([hi, lo, hi], axis=0)

    def expand(v):
        lanes = lax.broadcasted_iota(jnp.int32, v.shape, 1)
        hi, lo = split(v)

        def moved(x, by):
            return x if by == 0 else pltpu.roll(x, by % 128, 1)

        out = []
        for k in range(3):
            low = moved(hi, -RANK * k)
            mid = moved(lo, RANK - RANK * k)
            top = moved(hi, 2 * RANK - RANK * k)
            out.append(jnp.where(lanes < RANK, low, jnp.where(lanes < 2 * RANK, mid, top)))
        return out

    def smooth(phase):
        chunk = half // 2
        blank = jnp.zeros((128, half), BF)

        def pack(j, c):
            rows = slice(chunk * c, chunk * (c + 1))
            if phase == 0:
                first = dot(left[j, rows, :], coef3[...])
            else:
                rows = slice(chunk * (c % 2), chunk * (c % 2 + 1))
                first = dot(left_far[j, c // 2, rows, :], far3[c // 2])
            west, mid, east = (expand(first[:, 128 * t : 128 * (t + 1)]) for t in range(3))
            pairs = [jnp.concatenate([west[k], east[k]], axis=1) for k in range(3)]
            return jnp.concatenate(mid, axis=0), jnp.concatenate(pairs, axis=0)

        def add(j, c, mid, pairs):
            rows = slice(chunk * c, chunk * (c + 1))
            table = right[j]
            both = jnp.concatenate(
                [
                    jnp.concatenate([table[:, half:], blank], axis=1),
                    jnp.concatenate([blank, table[:, :half]], axis=1),
                ],
                axis=0,
            )
            for at, got in ((0, dot(mid, table)), (tile, dot(pairs, both))):
                new = None if j == 0 else win[phase, rows, at : at + tile]
                for k in range(3):
                    cut = GAIN * jnp.abs(weights[k]) * thr_ref[j, k]
                    term = soft(got[chunk * k : chunk * (k + 1)], cut)
                    new = term if new is None else new + term
                win[phase, rows, at : at + tile] = new

        def model(j):
            at = pl.multiple_of(me * slab, slab)
            mine = expand(dot(left[j, pl.ds(at, slab), :], own3[...]))
            got = dot(jnp.concatenate(mine, axis=0), right[j])
            for k in range(3):
                term = GAIN * soft(got[slab * k : slab * (k + 1)], thr_ref[j, k])
                model_out[k] += term

        items = [(j, c) for j in range(levels) for c in range(4)]
        packed = {}
        for step in range(0, len(items) + AHEAD, AHEAD):
            for i in range(step, step + AHEAD):
                if i >= AHEAD:
                    add(*items[i - AHEAD], *packed.pop(i - AHEAD))
                if i < len(items):
                    packed[i] = pack(*items[i])
            if phase == 0 and step < AHEAD * levels and step % AHEAD == 0:
                model(step // AHEAD)

    def masked(cyc, phase, bands_of_rows):
        rows = []
        for at, (dr, qr) in enumerate(bands_of_rows):
            blocks = []
            for (dc, qc), src in (((-1, 1), tile), ((0, 0), 0), ((0, 1), half), ((1, 0), tile + half)):
                q = 2 * qr + qc
                if dr == 0:
                    flag = sky_buf[cyc, near_slot(dc), q : q + 1, 127:128]
                else:
                    flag = far_in[cyc, far_slot(dr, dc), q : q + 1, 127:128]
                blocks.append(win[phase, half * at : half * (at + 1), src : src + half] * flag)
            rows.append(jnp.concatenate(blocks, axis=1))
        return split(jnp.concatenate(rows, axis=0))

    def cycle(cyc, carry):
        for d in range(1, bands):
            band_copy(cyc, d).wait_recv()
        sums = []
        for k in range(3):
            total = weights[k] * gather[cyc, 0]
            for d in range(1, bands):
                total = total + weight_ref[k, (me - d + bands) % bands] * gather[cyc, d]
            sums.append(total)
        groups = []
        for g in range(3):
            out = jnp.zeros((16, 128), F32)
            for k in range(3):
                moved = sums[k]
                if k != g:
                    moved = pltpu.roll(moved, (RANK * (k - g)) % 128, 1)
                ours = (lane16 >= RANK * k) & (lane16 < RANK * (k + 1))
                out = jnp.where(ours, moved, out)
            groups.append(out)
        full = jnp.concatenate(groups, axis=0)
        o_hi, o_lo = split(full)
        stacked = jnp.concatenate([o_hi, o_lo, o_hi], axis=0)
        less = dot(reduce[...], stacked)
        for i in range(2):
            far_out[cyc, i] = with_flags(less[FAR_RANK * i : FAR_RANK * (i + 1)])
        send(cyc, FAR)
        sky_buf[cyc, 0] = with_flags(full)
        send(cyc, NEAR)
        own3[...] = stacked
        place(coef3, 1, full)
        receive(cyc, NEAR)
        for dr, dc in NEAR:
            place(coef3, dc + 1, sky_buf[cyc, near_slot(dc)])
        smooth(0)
        w_hi, w_lo = masked(cyc, 0, [(0, 0), (0, 1)])
        inner = slice(half, half + tile)
        spec[...] = const_data(rows_fwd[0, :, inner], rows_fwd[1, :, inner], w_hi, w_lo)

        receive(cyc, FAR)
        for dr, dc in FAR:
            place(far3.at[(dr + 1) // 2], dc + 1, far_in[cyc, far_slot(dr, dc)])
        smooth(1)
        w_hi, w_lo = masked(cyc, 1, [(-1, 1), (1, 0)])

        w_rows = jnp.concatenate([w_hi, w_lo, w_hi], axis=0)
        part_rows = half

        def freqs(c):
            return [slice(at + part_rows * c, at + part_rows * (c + 1)) for at in (0, tile)]

        def start(c):
            def outer(part):
                return jnp.concatenate(
                    [
                        jnp.concatenate(
                            [rows_fwd[part, f, :half], rows_fwd[part, f, half + tile :]], axis=1
                        )
                        for f in freqs(c)
                    ],
                    axis=0,
                )

            hi = outer(0)
            got = dot(jnp.concatenate([hi, hi, outer(1)], axis=1), w_rows)
            re, im = (
                got[part_rows * i : part_rows * (i + 1)] + spec[f, :]
                for i, f in enumerate(freqs(c))
            )
            blocks = [[v[:, half * m : half * (m + 1)] for m in range(4)] for v in (re, im)]
            return [split(v) for v in residues(*blocks)]

        def along(pair, r):
            return data_const(*pair, cols[r, 0], cols[r, 1])

        def back(r, x):
            x_re, x_im = x[:, :half], x[:, half:]
            b_re, b_im = beam_f[r, :, :half], beam_f[r, :, half:]
            hi, lo = split(
                jnp.concatenate([x_re * b_re - x_im * b_im, x_re * b_im + x_im * b_re], axis=1)
            )
            return data_const(hi, lo, cols_t[r, 0], cols_t[r, 1])

        first, second = start(0), start(1)
        x, t = [], []
        for r in range(4):
            pair = [jnp.concatenate([first[r][i], second[r][i]], axis=0) for i in range(2)]
            x.append(along(pair, r))
            if r > 0:
                t.append(back(r - 1, x[r - 1]))
        t.append(back(3, x[3]))
        even, odd, gap, turn = t[0] + t[2], t[1] + t[3], t[0] - t[2], t[1] - t[3]
        z_re = jnp.concatenate(
            [even[:, :half] - odd[:, :half], gap[:, :half] + turn[:, half:]], axis=1
        )
        z_im = jnp.concatenate(
            [even[:, half:] - odd[:, half:], gap[:, half:] - turn[:, :half]], axis=1
        )
        z_hi, z_lo = split(jnp.concatenate([z_re, z_im], axis=0))
        res_out[...] = res_out[...] - const_data(rows_inv[0], rows_inv[1], z_hi, z_lo)

        @pl.when(cyc + 1 < CYCLES)
        def _():
            compress(cyc + 1)

        return carry

    lax.fori_loop(0, CYCLES, cycle, 0)
    for cyc in range(CYCLES):
        for d in range(1, bands):
            band_copy(cyc, d).wait_send()
        for dr, dc in NEAR + FAR:

            @pl.when(inside(dr, dc))
            def _():
                sky_copy(cyc, dr, dc).wait_send()


def finish(model_in, res_in, model_out, res_out):
    model_out[...] = model_in[...]
    res_out[...] = res_in[...]


def on_device(residual_start, beam_pattern, spec_weights, thresholds, block_ids, block_counts):
    bands = lax.axis_size("band")
    sky = lax.axis_size("sky")
    tile = residual_start.shape[-1]
    coefs = spec_weights.shape[1]
    levels = thresholds.shape[0]
    tables = host_tables(tile, levels)
    vmem = pl.BlockSpec(memory_space=pltpu.VMEM)
    hbm = pl.BlockSpec(memory_space=pl.ANY)
    region = 2 * tile
    shapes = (
        jax.ShapeDtypeStruct((coefs, tile // bands, tile), F32),
        jax.ShapeDtypeStruct((tile, tile), F32),
    )
    model, res = pl.pallas_call(
        functools.partial(kernel, bands, sky),
        out_shape=shapes,
        in_specs=[hbm] * 14,
        out_specs=(vmem, vmem),
        scratch_shapes=[
            pltpu.SMEM((4,), jnp.int32),
            pltpu.SMEM((1,), jnp.int32),
            pltpu.SMEM((coefs, bands), F32),
            pltpu.SMEM((levels, coefs), F32),
            pltpu.VMEM((tile, tile), F32),
        ]
        + [pltpu.VMEM(t.shape, BF) for t in tables]
        + [
            pltpu.VMEM((2, region, region), BF),
            pltpu.VMEM((2, tile, region), BF),
            pltpu.VMEM((4, 2, tile, tile), BF),
            pltpu.VMEM((CYCLES, bands, 16, 128), F32),
            pltpu.VMEM((CYCLES, 3, KPAD, 128), F32),
            pltpu.VMEM((CYCLES, 2, FAR_RANK, 128), F32),
            pltpu.VMEM((CYCLES, 6, FAR_RANK, 128), F32),
            pltpu.VMEM((3 * KPAD, 384), BF),
            pltpu.VMEM((2, 3 * FAR_RANK, 384), BF),
            pltpu.VMEM((3 * KPAD, 128), BF),
            pltpu.VMEM((2, tile, region), F32),
            pltpu.VMEM((region, region), F32),
            pltpu.VMEM((4, tile, tile), F32),
            pltpu.SemaphoreType.DMA((14,)),
            pltpu.SemaphoreType.DMA((CYCLES, bands)),
            pltpu.SemaphoreType.DMA((CYCLES, bands)),
            pltpu.SemaphoreType.DMA((CYCLES, 9)),
            pltpu.SemaphoreType.DMA((CYCLES, 9)),
        ],
        compiler_params=pltpu.CompilerParams(
            collective_id=0, has_side_effects=True, vmem_limit_bytes=32 << 20
        ),
    )(
        pltpu.with_memory_space_constraint(block_ids[0, 0], pltpu.HBM),
        block_counts[0],
        *[
            pltpu.with_memory_space_constraint(x, pltpu.HBM)
            for x in (
                spec_weights.T,
                thresholds,
                residual_start[0, 0],
                beam_pattern[0],
                *[jnp.asarray(t) for t in tables],
            )
        ],
    )
    model, res = pl.pallas_call(
        finish,
        out_shape=shapes,
        in_specs=[vmem] * 2,
        out_specs=(vmem, vmem),
        compiler_params=pltpu.CompilerParams(vmem_limit_bytes=4 << 20),
    )(model, res)
    return (model[:, None], res[None, None])


def solution(mesh):
    placed = (
        P("band", "sky", None, None),
        P("band", None, None),
        P(),
        P(),
        P("band", "sky", None),
        P("band", "sky"),
    )
    return jax.shard_map(
        on_device,
        mesh=mesh,
        in_specs=placed,
        out_specs=(P(None, "sky", "band", None), P("band", "sky", None, None)),
        check_vma=False,
    )
```

```python
import functools

import jax
import jax.numpy as jnp
import numpy as np
from jax import lax
from jax.experimental import pallas as pl
from jax.experimental.pallas import tpu as pltpu
from jax.sharding import PartitionSpec as P

CYCLES = 2
TGX = 4
GAIN = 0.25
RANK = 42
KPAD = 48
AHEAD = 4
FAR_RANK = 32
MESH = pl.DeviceIdType.MESH
BF = jnp.bfloat16
F32 = jnp.float32


def host_split(a):
    hi = np.asarray(a, np.float64).astype(BF)
    lo = (np.asarray(a, np.float64) - hi.astype(np.float64)).astype(BF)
    return hi, lo


def host_tables(tile, levels):
    pos = np.arange(tile, dtype=np.float64)
    off = pos[:, None] - pos[None, :]
    smooth = []
    for j in range(levels):
        spread = 2.0**j * tile / 16.0
        k = np.exp(-off * off / (2.0 * spread * spread))
        smooth.append(k / np.sqrt(np.sum(k * k, axis=1, keepdims=True)))
    smooth = np.stack(smooth)
    _, _, vt = np.linalg.svd(smooth.reshape(-1, tile), full_matrices=False)
    basis = vt[:RANK].T
    proj = np.zeros((tile, 128))
    proj[:, :RANK] = basis
    proj_t = np.zeros((KPAD, tile))
    proj_t[:RANK] = basis.T
    expand = smooth @ basis

    p_hi, p_lo = host_split(proj)
    t_hi, t_lo = host_split(proj_t)
    project = np.concatenate([p_hi, p_hi, p_lo], axis=0)
    project_t = np.concatenate([t_hi, t_hi, t_lo], axis=1)

    left = np.zeros((levels, tile, KPAD))
    left[:, :, :RANK] = expand
    l_hi, l_lo = host_split(left)
    left3 = np.concatenate([l_hi, l_hi, l_lo], axis=2)

    far, reduce = [], np.zeros((2 * FAR_RANK, KPAD))
    for i, rows in enumerate((slice(tile // 2, tile), slice(0, tile // 2))):
        _, _, vt = np.linalg.svd(expand[:, rows].reshape(-1, RANK), full_matrices=False)
        reduce[FAR_RANK * i : FAR_RANK * (i + 1), :RANK] = vt[:FAR_RANK]
        f_hi, f_lo = host_split(expand[:, rows] @ vt[:FAR_RANK].T)
        far.append(np.concatenate([f_hi, f_hi, f_lo], axis=2))
    left_far = np.stack(far, axis=1)
    z_hi, z_lo = host_split(reduce)
    reduce3 = np.concatenate([z_hi, z_hi, z_lo], axis=1)

    right = np.zeros((levels, 128, tile), BF)
    g_hi, g_lo = host_split(expand.transpose(0, 2, 1))
    for p, g in enumerate((g_hi, g_hi, g_lo)):
        right[:, RANK * p : RANK * (p + 1)] = g

    n = 2 * tile
    f = np.arange(tile) + 0.5
    ang = 2.0 * np.pi * f[:, None] * np.arange(tile)[None, :] / n
    rows_fwd = np.stack(host_split(np.concatenate([np.cos(ang), -np.sin(ang)], axis=0)))

    cols = []
    x = np.arange(tile // 2)
    for r in range(4):
        a = 2.0 * np.pi * x[:, None] * (4 * x[None, :] + r) / n
        c, s = np.cos(a), np.sin(a)
        cols.append(np.stack(host_split(np.block([[c, -s], [s, c]]))))
    cols = np.stack(cols)
    return project_t, project, reduce3, rows_fwd, cols, left3, right, left_far


def split(v):
    hi = v.astype(BF)
    return hi, (v - hi.astype(F32)).astype(BF)


def dot(a, b):
    return jnp.dot(a, b, preferred_element_type=F32)


def data_const(hi, lo, c_hi, c_lo):
    return dot(jnp.concatenate([hi, lo, hi], axis=1), jnp.concatenate([c_hi, c_hi, c_lo], axis=0))


def const_data(c_hi, c_lo, hi, lo):
    return dot(jnp.concatenate([c_hi, c_hi, c_lo], axis=1), jnp.concatenate([hi, lo, hi], axis=0))


def soft(v, t):
    return v - jnp.minimum(jnp.maximum(v, -t), t)


def residues(re, im):
    (a_re, b_re, c_re, d_re), (a_im, b_im, c_im, d_im) = (
        (v[0] + v[2], v[1] + v[3], v[0] - v[2], v[1] - v[3]) for v in (re, im)
    )
    return [
        jnp.concatenate(pair, axis=1)
        for pair in (
            (a_re + b_re, a_im + b_im),
            (c_re + d_im, c_im - d_re),
            (a_re - b_re, a_im - b_im),
            (c_re - d_im, c_im + d_re),
        )
    ]


NEAR = [(0, 1), (0, -1)]
FAR = [(1, 0), (-1, 0), (1, 1), (1, -1), (-1, 1), (-1, -1)]


def kernel(
    bands,
    sky,
    ids_hbm,
    count_hbm,
    weight_hbm,
    thr_hbm,
    res_hbm,
    beam_hbm,
    project_t_hbm,
    project_hbm,
    reduce_hbm,
    rows_hbm,
    cols_hbm,
    left_hbm,
    right_hbm,
    left_far_hbm,
    model_out,
    res_out,
    ids_ref,
    count_ref,
    weight_ref,
    thr_ref,
    beam,
    project_t,
    project,
    reduce,
    rows_half,
    cols,
    left,
    right,
    left_far,
    rows_fwd,
    rows_inv,
    cols_t,
    gather,
    sky_buf,
    far_out,
    far_in,
    coef3,
    far3,
    own3,
    win,
    spec,
    beam_f,
    const_sem,
    band_send,
    band_recv,
    sky_send,
    sky_recv,
):
    tile = res_out.shape[0]
    half = tile // 2
    levels = left.shape[0]
    slab = tile // bands
    sky_rows = sky // TGX
    me = lax.axis_index("band")
    spot = lax.axis_index("sky")
    row, col = spot // TGX, spot % TGX

    def sky_id(dr, dc):
        return ((row + dr + sky_rows) % sky_rows) * TGX + (col + dc + TGX) % TGX

    pairs = [
        (res_hbm, res_out),
        (project_t_hbm, project_t),
        (project_hbm, project),
        (beam_hbm, beam),
        (rows_hbm, rows_half),
        (cols_hbm, cols),
        (reduce_hbm, reduce),
        (left_hbm, left),
        (right_hbm, right),
        (left_far_hbm, left_far),
        (ids_hbm, ids_ref),
        (count_hbm, count_ref),
        (weight_hbm, weight_ref),
        (thr_hbm, thr_ref),
    ]
    copies = [
        pltpu.make_async_copy(src, dst, const_sem.at[i]) for i, (src, dst) in enumerate(pairs)
    ]
    for copy in copies[:3]:
        copy.start()

    barrier = pltpu.get_barrier_semaphore()
    for d in range(1, bands):
        pl.semaphore_signal(
            barrier, inc=1, device_id={"band": (me + d) % bands}, device_id_type=MESH
        )
    for dr, dc in NEAR + FAR:
        pl.semaphore_signal(barrier, inc=1, device_id={"sky": sky_id(dr, dc)}, device_id_type=MESH)

    for copy in copies[3:]:
        copy.start()

    def band_copy(cyc, d):
        return pltpu.make_async_remote_copy(
            src_ref=gather.at[cyc, 0],
            dst_ref=gather.at[cyc, d],
            send_sem=band_send.at[cyc, d],
            recv_sem=band_recv.at[cyc, d],
            device_id={"band": (me + d) % bands},
            device_id_type=MESH,
        )

    def compress(cyc):
        r_hi, r_lo = split(res_out[...])
        part = dot(project_t[...], jnp.concatenate([r_hi, r_lo, r_hi], axis=0))
        p_hi, p_lo = split(part)
        coef = dot(jnp.concatenate([p_hi, p_lo, p_hi], axis=1), project[...])
        gather[cyc, 0] = (
            coef[0:16] + pltpu.roll(coef[16:32], RANK, 1) + pltpu.roll(coef[32:48], 2 * RANK, 1)
        )
        if isinstance(cyc, int):
            pl.semaphore_wait(barrier, bands - 1 + 8)
        for d in range(1, bands):
            band_copy(cyc, d).start()

    for copy in copies[:3]:
        copy.wait()
    compress(0)

    model_out[...] = jnp.zeros_like(model_out)

    lane = lax.broadcasted_iota(jnp.int32, (1, 128), 1)
    lane16 = lax.broadcasted_iota(jnp.int32, (16, 128), 1)
    for copy in copies[10:]:
        copy.wait()
    flags = []
    for q in range(4):
        live = jnp.float32(0.0)
        for s in range(4):
            hit = jnp.where(ids_ref[s] == q, 1.0, 0.0) * jnp.where(s < count_ref[0], 1.0, 0.0)
            live = live + hit
        flags.append(live)
    weights = [weight_ref[k, me] for k in range(3)]
    scale = jnp.zeros((1, 128), F32)
    for k in range(3):
        ours = (lane >= RANK * k) & (lane < RANK * (k + 1))
        scale = jnp.where(ours, GAIN * weights[k], scale)

    def near_slot(dc):
        return (dc + 3) % 3

    def sky_copy(cyc, dr, dc):
        if dr == 0:
            src, dst = sky_buf.at[cyc, 0], sky_buf.at[cyc, near_slot(-dc)]
        else:
            src, dst = far_out.at[cyc, (1 - dr) // 2], far_in.at[cyc, far_slot(-dr, -dc)]
        slot = (1 - dr) * 3 + (1 - dc)
        return pltpu.make_async_remote_copy(
            src_ref=src,
            dst_ref=dst,
            send_sem=sky_send.at[cyc, slot],
            recv_sem=sky_recv.at[cyc, slot],
            device_id={"sky": sky_id(dr, dc)},
            device_id_type=MESH,
        )

    def far_slot(dr, dc):
        return (dr + 1) // 2 * 3 + dc + 1

    def inside(dr, dc):
        return (row + dr >= 0) & (row + dr < sky_rows) & (col + dc >= 0) & (col + dc < TGX)

    for dr, dc in NEAR + FAR:

        @pl.when(jnp.logical_not(inside(dr, dc)))
        def _():
            for cyc in range(CYCLES):
                if dr == 0:
                    sky_buf[cyc, near_slot(dc)] = jnp.zeros((KPAD, 128), F32)
                else:
                    far_in[cyc, far_slot(dr, dc)] = jnp.zeros((FAR_RANK, 128), F32)

    def send(cyc, where):
        for dr, dc in where:

            @pl.when(inside(dr, dc))
            def _():
                sky_copy(cyc, dr, dc).start()

    def receive(cyc, where):
        for dr, dc in where:

            @pl.when(inside(dr, dc))
            def _():
                sky_copy(cyc, -dr, -dc).wait_recv()

    def with_flags(v):
        r = lax.broadcasted_iota(jnp.int32, v.shape, 0)
        c = lax.broadcasted_iota(jnp.int32, v.shape, 1)
        for q in range(4):
            v = jnp.where((c == 127) & (r == q), flags[q], v)
        return v

    def prepare():
        for copy in copies[3:6]:
            copy.wait()
        alt = (1 - 2 * (lax.broadcasted_iota(jnp.int32, (tile, 1), 0) % 2)).astype(F32)
        b_hi, b_lo = split(beam[...])
        first = const_data(rows_half[0], rows_half[1], b_hi, b_lo)
        blank = jnp.zeros((tile, half), F32)
        re, im = (
            [first[at : at + tile, :half], first[at : at + tile, half:], blank, blank]
            for at in (0, tile)
        )
        norm = 2.0 / (4 * tile * tile)
        for r, v in enumerate(residues(re, im)):
            hi, lo = split(v)
            beam_f[r] = norm * data_const(hi, lo, cols[r, 0], cols[r, 1])
        for part in range(2):
            re = rows_half[part, :tile].astype(F32)
            im = rows_half[part, tile:].astype(F32)
            re_far, im_far = im * alt, -(re * alt)
            rows_fwd[part, :, :tile] = rows_half[part]
            rows_fwd[part, :tile, tile:] = re_far.astype(BF)
            rows_fwd[part, tile:, tile:] = im_far.astype(BF)
            rows_inv[part, :, :tile] = re_far.T.astype(BF)
            rows_inv[part, :, tile:] = im_far.T.astype(BF)
            for r in range(4):
                cols_t[r, part] = cols[r, part].astype(F32).T.astype(BF)
        for copy in copies[6:10]:
            copy.wait()

    prepare()

    def place(dst, lanes, v):
        hi, lo = split(v * scale)
        dst[:, 128 * lanes : 128 * (lanes + 1)] = jnp.concatenate([hi, lo, hi], axis=0)

    def expand(v):
        lanes = lax.broadcasted_iota(jnp.int32, v.shape, 1)
        hi, lo = split(v)

        def moved(x, by):
            return x if by == 0 else pltpu.roll(x, by % 128, 1)

        out = []
        for k in range(3):
            low = moved(hi, -RANK * k)
            mid = moved(lo, RANK - RANK * k)
            top = moved(hi, 2 * RANK - RANK * k)
            out.append(jnp.where(lanes < RANK, low, jnp.where(lanes < 2 * RANK, mid, top)))
        return out

    def smooth(phase):
        chunk = half // 2
        blank = jnp.zeros((128, half), BF)

        def pack(j, c):
            rows = slice(chunk * c, chunk * (c + 1))
            if phase == 0:
                first = dot(left[j, rows, :], coef3[...])
            else:
                rows = slice(chunk * (c % 2), chunk * (c % 2 + 1))
                first = dot(left_far[j, c // 2, rows, :], far3[c // 2])
            west, mid, east = (expand(first[:, 128 * t : 128 * (t + 1)]) for t in range(3))
            pairs = [jnp.concatenate([west[k], east[k]], axis=1) for k in range(3)]
            return jnp.concatenate(mid, axis=0), jnp.concatenate(pairs, axis=0)

        def add(j, c, mid, pairs):
            rows = slice(chunk * c, chunk * (c + 1))
            table = right[j]
            both = jnp.concatenate(
                [
                    jnp.concatenate([table[:, half:], blank], axis=1),
                    jnp.concatenate([blank, table[:, :half]], axis=1),
                ],
                axis=0,
            )
            for at, got in ((0, dot(mid, table)), (tile, dot(pairs, both))):
                new = None if j == 0 else win[phase, rows, at : at + tile]
                for k in range(3):
                    cut = GAIN * jnp.abs(weights[k]) * thr_ref[j, k]
                    term = soft(got[chunk * k : chunk * (k + 1)], cut)
                    new = term if new is None else new + term
                win[phase, rows, at : at + tile] = new

        def model(j):
            at = pl.multiple_of(me * slab, slab)
            mine = expand(dot(left[j, pl.ds(at, slab), :], own3[...]))
            got = dot(jnp.concatenate(mine, axis=0), right[j])
            for k in range(3):
                term = GAIN * soft(got[slab * k : slab * (k + 1)], thr_ref[j, k])
                model_out[k] += term

        items = [(j, c) for j in range(levels) for c in range(4)]
        packed = {}
        for step in range(0, len(items) + AHEAD, AHEAD):
            for i in range(step, step + AHEAD):
                if i >= AHEAD:
                    add(*items[i - AHEAD], *packed.pop(i - AHEAD))
                if i < len(items):
                    packed[i] = pack(*items[i])
            if phase == 0 and step < AHEAD * levels and step % AHEAD == 0:
                model(step // AHEAD)

    def masked(cyc, phase, bands_of_rows):
        rows = []
        for at, (dr, qr) in enumerate(bands_of_rows):
            blocks = []
            for (dc, qc), src in (((-1, 1), tile), ((0, 0), 0), ((0, 1), half), ((1, 0), tile + half)):
                q = 2 * qr + qc
                if dr == 0:
                    flag = sky_buf[cyc, near_slot(dc), q : q + 1, 127:128]
                else:
                    flag = far_in[cyc, far_slot(dr, dc), q : q + 1, 127:128]
                blocks.append(win[phase, half * at : half * (at + 1), src : src + half] * flag)
            rows.append(jnp.concatenate(blocks, axis=1))
        return split(jnp.concatenate(rows, axis=0))

    def cycle(cyc, carry):
        for d in range(1, bands):
            band_copy(cyc, d).wait_recv()
        sums = []
        for k in range(3):
            total = weights[k] * gather[cyc, 0]
            for d in range(1, bands):
                total = total + weight_ref[k, (me - d + bands) % bands] * gather[cyc, d]
            sums.append(total)
        groups = []
        for g in range(3):
            out = jnp.zeros((16, 128), F32)
            for k in range(3):
                moved = sums[k]
                if k != g:
                    moved = pltpu.roll(moved, (RANK * (k - g)) % 128, 1)
                ours = (lane16 >= RANK * k) & (lane16 < RANK * (k + 1))
                out = jnp.where(ours, moved, out)
            groups.append(out)
        full = jnp.concatenate(groups, axis=0)
        o_hi, o_lo = split(full)
        stacked = jnp.concatenate([o_hi, o_lo, o_hi], axis=0)
        less = dot(reduce[...], stacked)
        for i in range(2):
            far_out[cyc, i] = with_flags(less[FAR_RANK * i : FAR_RANK * (i + 1)])
        send(cyc, FAR)
        sky_buf[cyc, 0] = with_flags(full)
        send(cyc, NEAR)
        own3[...] = stacked
        place(coef3, 1, full)
        receive(cyc, NEAR)
        for dr, dc in NEAR:
            place(coef3, dc + 1, sky_buf[cyc, near_slot(dc)])
        smooth(0)
        w_hi, w_lo = masked(cyc, 0, [(0, 0), (0, 1)])
        inner = slice(half, half + tile)
        spec[...] = const_data(rows_fwd[0, :, inner], rows_fwd[1, :, inner], w_hi, w_lo)

        receive(cyc, FAR)
        for dr, dc in FAR:
            place(far3.at[(dr + 1) // 2], dc + 1, far_in[cyc, far_slot(dr, dc)])
        smooth(1)
        w_hi, w_lo = masked(cyc, 1, [(-1, 1), (1, 0)])

        w_rows = jnp.concatenate([w_hi, w_lo, w_hi], axis=0)
        part_rows = half

        def freqs(c):
            return [slice(at + part_rows * c, at + part_rows * (c + 1)) for at in (0, tile)]

        def start(c):
            def outer(part):
                return jnp.concatenate(
                    [
                        jnp.concatenate(
                            [rows_fwd[part, f, :half], rows_fwd[part, f, half + tile :]], axis=1
                        )
                        for f in freqs(c)
                    ],
                    axis=0,
                )

            hi = outer(0)
            got = dot(jnp.concatenate([hi, hi, outer(1)], axis=1), w_rows)
            re, im = (
                got[part_rows * i : part_rows * (i + 1)] + spec[f, :]
                for i, f in enumerate(freqs(c))
            )
            blocks = [[v[:, half * m : half * (m + 1)] for m in range(4)] for v in (re, im)]
            return [split(v) for v in residues(*blocks)]

        def along(pair, r):
            return data_const(*pair, cols[r, 0], cols[r, 1])

        def back(r, x):
            x_re, x_im = x[:, :half], x[:, half:]
            b_re, b_im = beam_f[r, :, :half], beam_f[r, :, half:]
            hi, lo = split(
                jnp.concatenate([x_re * b_re - x_im * b_im, x_re * b_im + x_im * b_re], axis=1)
            )
            return data_const(hi, lo, cols_t[r, 0], cols_t[r, 1])

        first, second = start(0), start(1)
        x, t = [], []
        for r in range(4):
            pair = [jnp.concatenate([first[r][i], second[r][i]], axis=0) for i in range(2)]
            x.append(along(pair, r))
            if r > 0:
                t.append(back(r - 1, x[r - 1]))
        t.append(back(3, x[3]))
        even, odd, gap, turn = t[0] + t[2], t[1] + t[3], t[0] - t[2], t[1] - t[3]
        z_re = jnp.concatenate(
            [even[:, :half] - odd[:, :half], gap[:, :half] + turn[:, half:]], axis=1
        )
        z_im = jnp.concatenate(
            [even[:, half:] - odd[:, half:], gap[:, half:] - turn[:, :half]], axis=1
        )
        z_hi, z_lo = split(jnp.concatenate([z_re, z_im], axis=0))
        res_out[...] = res_out[...] - const_data(rows_inv[0], rows_inv[1], z_hi, z_lo)

        @pl.when(cyc + 1 < CYCLES)
        def _():
            compress((cyc + 1) % CYCLES)

        return carry

    lax.fori_loop(0, CYCLES, cycle, 0)
    for cyc in range(CYCLES):
        for d in range(1, bands):
            band_copy(cyc, d).wait_send()
        for dr, dc in NEAR + FAR:

            @pl.when(inside(dr, dc))
            def _():
                sky_copy(cyc, dr, dc).wait_send()


def finish(model_in, res_in, model_out, res_out):
    model_out[...] = model_in[...]
    res_out[...] = res_in[...]


def on_device(residual_start, beam_pattern, spec_weights, thresholds, block_ids, block_counts):
    bands = lax.axis_size("band")
    sky = lax.axis_size("sky")
    tile = residual_start.shape[-1]
    coefs = spec_weights.shape[1]
    levels = thresholds.shape[0]
    tables = host_tables(tile, levels)
    vmem = pl.BlockSpec(memory_space=pltpu.VMEM)
    hbm = pl.BlockSpec(memory_space=pl.ANY)
    region = 2 * tile
    shapes = (
        jax.ShapeDtypeStruct((coefs, tile // bands, tile), F32),
        jax.ShapeDtypeStruct((tile, tile), F32),
    )
    model, res = pl.pallas_call(
        functools.partial(kernel, bands, sky),
        out_shape=shapes,
        in_specs=[hbm] * 14,
        out_specs=(vmem, vmem),
        scratch_shapes=[
            pltpu.SMEM((4,), jnp.int32),
            pltpu.SMEM((1,), jnp.int32),
            pltpu.SMEM((coefs, bands), F32),
            pltpu.SMEM((levels, coefs), F32),
            pltpu.VMEM((tile, tile), F32),
        ]
        + [pltpu.VMEM(t.shape, BF) for t in tables]
        + [
            pltpu.VMEM((2, region, region), BF),
            pltpu.VMEM((2, tile, region), BF),
            pltpu.VMEM((4, 2, tile, tile), BF),
            pltpu.VMEM((CYCLES, bands, 16, 128), F32),
            pltpu.VMEM((CYCLES, 3, KPAD, 128), F32),
            pltpu.VMEM((CYCLES, 2, FAR_RANK, 128), F32),
            pltpu.VMEM((CYCLES, 6, FAR_RANK, 128), F32),
            pltpu.VMEM((3 * KPAD, 384), BF),
            pltpu.VMEM((2, 3 * FAR_RANK, 384), BF),
            pltpu.VMEM((3 * KPAD, 128), BF),
            pltpu.VMEM((2, tile, region), F32),
            pltpu.VMEM((region, region), F32),
            pltpu.VMEM((4, tile, tile), F32),
            pltpu.SemaphoreType.DMA((14,)),
            pltpu.SemaphoreType.DMA((CYCLES, bands)),
            pltpu.SemaphoreType.DMA((CYCLES, bands)),
            pltpu.SemaphoreType.DMA((CYCLES, 9)),
            pltpu.SemaphoreType.DMA((CYCLES, 9)),
        ],
        compiler_params=pltpu.CompilerParams(
            collective_id=0, has_side_effects=True, vmem_limit_bytes=32 << 20
        ),
    )(
        pltpu.with_memory_space_constraint(block_ids[0, 0], pltpu.HBM),
        block_counts[0],
        *[
            pltpu.with_memory_space_constraint(x, pltpu.HBM)
            for x in (
                spec_weights.T,
                thresholds,
                residual_start[0, 0],
                beam_pattern[0],
                *[jnp.asarray(t) for t in tables],
            )
        ],
    )
    model, res = pl.pallas_call(
        finish,
        out_shape=shapes,
        in_specs=[vmem] * 2,
        out_specs=(vmem, vmem),
        compiler_params=pltpu.CompilerParams(vmem_limit_bytes=4 << 20),
    )(model, res)
    return (model[:, None], res[None, None])


def solution(mesh):
    placed = (
        P("band", "sky", None, None),
        P("band", None, None),
        P(),
        P(),
        P("band", "sky", None),
        P("band", "sky"),
    )
    return jax.shard_map(
        on_device,
        mesh=mesh,
        in_specs=placed,
        out_specs=(P(None, "sky", "band", None), P("band", "sky", None, None)),
        check_vma=False,
    )
```
